128 devices in a mesh: frag: 4 (over y_hi, core), aux: 16 (over z, x), orb: 2 (over y_lo).
Axes of the slice: x: 4, y: 4 (y_hi: 2, y_lo: 2; y = y_hi * 2 + y_lo), z: 4, core: 2. Of those that a mesh axis runs over, the one named last changes fastest.
Arguments:
- density: bfloat16 [16384, 2, 8192], P('frag', 'orb', 'aux'), may hold values from -0.046875 to 0.046875
- bath: bfloat16 [16, 2, 8192, 128], P('frag', 'orb', 'aux'), may hold values from -1 to 1
- factor: bfloat16 [16384, 16384], P('orb', 'aux'), may hold values from -6 to 6
- frag_index: int32 [16, 128], replicated, may hold values from 0 to 16383, as said below
- nfrag: int32 [16], replicated, may hold values from 1 to 128
- nbath: int32 [16], replicated, may hold values from 1 to 128
Outputs:
- projected: bfloat16 [16, 256, 16384], P('frag', 'orb', 'aux')
The draws below stay inside these ranges and needn't reach their ends.
Inputs may be any that keep to these rules, and one draw needn't show every extreme that they name: `frag_index`: the 128 entries of one fragment's row are distinct basis functions; entries at or past nfrag are not read.
All inputs are finite; a program needn't handle non-finite values.
Results may differ from the reference program's by a relative error of at most 0.0049.
Values may be sent and summed in bfloat16 or wider, within the bound.
A program may use at most 128 MiB of HBM per device.

```python
import jax
import jax.numpy as jnp
from jax import lax

NBAS = 16384
NFMAX = 128
NBMAX = 128
NOCC = 16
FRAGS = 16
KMAX = 256
QTOT = 1024
N_ORB = 2


def draw_frag_index(key, part):
    keys = jax.random.split(jax.random.fold_in(key, 11), FRAGS)

    def pick_rows(one_key):
        return jax.random.permutation(one_key, NBAS)[:NFMAX].astype(jnp.int32)
    return jax.vmap(pick_rows)(keys)


def draw_bath(key, part):
    keys = jax.random.split(jax.random.fold_in(key, 23), 2)
    scales = jnp.exp(jax.random.uniform(keys[1], (FRAGS, 1, NBMAX), jnp.float32, -1.2, 1.2))
    base = jax.random.normal(keys[0], (FRAGS, NBAS, NBMAX), jnp.float32)
    values = base * scales * NBAS ** (-0.5)
    return values.reshape(FRAGS, N_ORB, NBAS // N_ORB, NBMAX).astype(jnp.bfloat16)


def place_ends(array, own_key, smallest, largest):
    dims = array.shape
    place = [jax.random.randint(jax.random.fold_in(own_key, axis), (), 0, dims[axis]) for axis in range(len(dims))]
    array = array.at[tuple(place)].set(smallest)
    longest = dims.index(max(dims))
    place[longest] = (place[longest] + 1) % dims[longest]
    return array.at[tuple(place)].set(largest)


def levels(stream_key, shape, cuts, low, largest):
    def one(position, parts):
        heights = jax.random.uniform(jax.random.fold_in(jax.random.fold_in(stream_key, 6), position), (parts,), jnp.float32, low / len(cuts), largest / len(cuts))
        return jnp.repeat(jnp.exp(heights), shape[position] // parts).reshape((-1,) + (1,) * (len(shape) - position - 1))

    gain = one(*cuts[0])
    for cut in cuts[1:]:
        gain = gain * one(*cut)
    return gain


def centred(stream_key, shape, deviation, most, shards=(), kind=jnp.bfloat16):
    result = jax.random.normal(stream_key, shape, jnp.float32) * deviation
    if len(shards) > 0:
        result = levels(stream_key, shape, shards, -0.22, 0.18) * result
    return jnp.clip(result, min=-most, max=most).astype(kind)


def setup_inputs(seed: int = 0) -> dict:
    arg_keys = jax.random.split(jax.random.key(seed), 7)
    return {
        "density": centred(arg_keys[0], (NBAS, N_ORB, NBAS // N_ORB), NBAS ** -0.5, 0.046875, ((0, 4), (1, 2), (2, 16))),
        "bath": draw_bath(jax.random.fold_in(arg_keys[6], 71), 0),
        "factor": centred(arg_keys[2], (NBAS, QTOT * NOCC), 1.0, 6.0, ((0, 2), (1, 16))),
        "frag_index": draw_frag_index(jax.random.fold_in(arg_keys[6], 71), 0),
        "nfrag": place_ends(jax.random.randint(arg_keys[4], (FRAGS,), 1, NFMAX + 1), jax.random.fold_in(arg_keys[4], 1), 1, NFMAX).astype(jnp.int32),
        "nbath": place_ends(jax.random.randint(arg_keys[5], (FRAGS,), 1, NBMAX + 1), jax.random.fold_in(arg_keys[5], 1), 1, NBMAX).astype(jnp.int32),
    }


def reference(density, bath, factor, frag_index, nfrag, nbath):
    density_full = density.reshape(NBAS, NBAS)
    bath_cols = bath.reshape(FRAGS, NBAS, NBMAX)
    frag_live = jnp.arange(NFMAX, dtype=jnp.int32)[None, :] < nfrag[:, None]
    bath_live = jnp.arange(NBMAX, dtype=jnp.int32)[None, :] < nbath[:, None]
    picked = jnp.take(density_full, frag_index.reshape(-1).astype(jnp.int32), axis=0)
    picked = picked.reshape(FRAGS, NFMAX, NBAS)
    picked = jnp.where(frag_live[:, :, None], picked, jnp.zeros_like(picked))
    bath_cols = jnp.where(bath_live[:, None, :], bath_cols, jnp.zeros_like(bath_cols))
    initial = jnp.concatenate([jnp.swapaxes(picked, 1, 2), bath_cols], axis=2)
    live_cols = jnp.concatenate([frag_live, bath_live], axis=1).astype(jnp.float32)
    initial_wide = initial.astype(jnp.float32)
    gram_total = jnp.einsum('fmk,fml->fkl', initial_wide, initial_wide, precision=lax.Precision.HIGHEST)
    gram_total = gram_total + jnp.eye(KMAX, dtype=jnp.float32)[None] * (1.0 - live_cols)[:, :, None]
    cholesky_low = jnp.linalg.cholesky(gram_total)
    coeffs = lax.linalg.triangular_solve(cholesky_low, initial_wide, left_side=False, lower=True, transpose_a=True)
    coeffs = coeffs.astype(jnp.bfloat16)

    def project(coeff_one):
        return jnp.dot(coeff_one.T.astype(jnp.float32), factor.astype(jnp.float32), preferred_element_type=jnp.float32).astype(jnp.bfloat16)
    return lax.map(project, coeffs)
```

```python
import jax
import jax.numpy as jnp
from jax import lax
from jax.experimental import pallas as pl
from jax.experimental.pallas import tpu as pltpu
from jax.sharding import PartitionSpec as P

HIGH = lax.Precision.HIGHEST
BLOCK = 64


def invert_tiles(tile_ref):
    shape = (BLOCK, 2 * BLOCK)
    lane = lax.broadcasted_iota(jnp.int32, shape, 1)
    row = lax.broadcasted_iota(jnp.int32, shape, 0)
    inner = lane % BLOCK
    start = lane - inner

    def step(j, carry):
        for pair in range(tile_ref.shape[0]):
            tile = tile_ref[pair]
            pivot_row = jnp.broadcast_to(tile_ref[pair, pl.ds(j, 1), :], (8, 2 * BLOCK))
            pivot = jnp.take_along_axis(pivot_row, start[:8] + j, axis=1)
            scaled = jnp.where(inner[:8] == j, 1.0, pivot_row) / pivot
            column = jnp.take_along_axis(tile, start + j, axis=1)
            scaled = jnp.broadcast_to(scaled[:1], shape)
            kept = jnp.where(inner == j, 0.0, tile)
            tile_ref[pair] = jnp.where(row > j, kept - column * scaled, tile)
        return carry

    lax.fori_loop(0, BLOCK, step, 0)
    for pair in range(tile_ref.shape[0]):
        tile = tile_ref[pair]
        pivots = jnp.take_along_axis(tile, start + row, axis=1)
        unit = jnp.where(inner < row, tile, jnp.where(inner == row, 1.0, 0.0))
        tile_ref[pair] = unit * lax.rsqrt(pivots)


def inverse_factor(work_ref, tile_ref):
    frags, size, _ = work_ref.shape
    for block in range(size // BLOCK):
        lo, hi = block * BLOCK, (block + 1) * BLOCK
        for f in range(frags):
            left = (f % 2) * BLOCK
            tile_ref[f // 2, :, left : left + BLOCK] = work_ref[f, lo:hi, lo:hi]
        invert_tiles(tile_ref)
        for f in range(frags):
            left = (f % 2) * BLOCK
            inverse = tile_ref[f // 2, :, left : left + BLOCK]
            rows = jnp.dot(inverse, work_ref[f, lo:hi, :], precision=HIGH, preferred_element_type=jnp.float32)
            work_ref[f, lo:hi, :] = rows
            work_ref[f, lo:hi, lo:hi] = inverse
            if hi < size:
                below = jnp.transpose(rows)[hi:, :]
                work_ref[f, hi:, lo:hi] = jnp.zeros((size - hi, BLOCK), jnp.float32)
                work_ref[f, hi:, :] -= jnp.dot(
                    below, work_ref[f, lo:hi, :], precision=HIGH, preferred_element_type=jnp.float32
                )


def factor_kernel(gram_ref, live_col_ref, live_row_ref, out_ref, work_ref, tile_ref):
    frags, size, _ = gram_ref.shape
    row = lax.broadcasted_iota(jnp.int32, (size, size), 0)
    col = lax.broadcasted_iota(jnp.int32, (size, size), 1)
    for f in range(frags):
        both = live_col_ref[f] * live_row_ref[f]
        work_ref[f] = jnp.where(both > 0.5, gram_ref[f], jnp.where(row == col, 1.0, 0.0))
    inverse_factor(work_ref, tile_ref)
    for f in range(frags):
        both = live_col_ref[f] * live_row_ref[f]
        out_ref[f] = jnp.where((both > 0.5) & (row >= col), work_ref[f], 0.0)


def inverse_of(gram, live_cols):
    frags, size, _ = gram.shape
    return pl.pallas_call(
        factor_kernel,
        out_shape=jax.ShapeDtypeStruct(gram.shape, jnp.float32),
        in_specs=[pl.BlockSpec(memory_space=pltpu.VMEM)] * 3,
        out_specs=pl.BlockSpec(memory_space=pltpu.VMEM),
        scratch_shapes=[
            pltpu.VMEM((frags, size, size), jnp.float32),
            pltpu.VMEM((frags // 2, BLOCK, 2 * BLOCK), jnp.float32),
        ],
    )(gram, live_cols[:, :, None], live_cols[:, None, :])


def per_device(density, bath, factor, frag_index, nfrag, nbath):
    local_rows = density.shape[0]
    block_cols = density.shape[2]
    density_local = density.reshape(local_rows, block_cols)
    group_size = bath.shape[0]
    frag_max = frag_index.shape[1]
    bath_max = bath.shape[3]
    frag_count = frag_index.shape[0]
    row_offset = lax.axis_index("frag") * local_rows
    local_index = frag_index - row_offset
    owned_rows = (local_index >= 0) & (local_index < local_rows)
    picked = jnp.take(density_local, jnp.clip(local_index, 0, local_rows - 1).reshape(-1), axis=0)
    picked = picked.reshape(frag_count, frag_max, block_cols)
    picked = jnp.where(owned_rows[:, :, None], picked, jnp.zeros_like(picked))
    rows = lax.psum_scatter(picked, "frag", scatter_dimension=0, tiled=True)
    first_frag = lax.axis_index("frag") * group_size
    my_nfrag = lax.dynamic_slice_in_dim(nfrag, first_frag, group_size)
    my_nbath = lax.dynamic_slice_in_dim(nbath, first_frag, group_size)
    frag_live = jnp.arange(frag_max, dtype=jnp.int32)[None, :] < my_nfrag[:, None]
    bath_live = jnp.arange(bath_max, dtype=jnp.int32)[None, :] < my_nbath[:, None]
    live_cols = jnp.concatenate([frag_live, bath_live], axis=1).astype(jnp.float32)
    bath_rows = jnp.swapaxes(bath.reshape(group_size, block_cols, bath_max), 1, 2)
    initial = jnp.concatenate([rows, bath_rows], axis=1)
    full = lax.all_gather(initial, "aux", axis=2, tiled=True)
    gram = jnp.einsum("fkm,flm->fkl", full, full, preferred_element_type=jnp.float32)
    gram = lax.psum(gram, "orb")
    inverse = inverse_of(gram, live_cols)
    partial_value = jnp.einsum("fkm,mq->fkq", full, factor, preferred_element_type=jnp.float32)
    value = jnp.einsum("fkl,flq->fkq", inverse, partial_value, precision=HIGH)
    summed = lax.psum_scatter(value.astype(jnp.bfloat16), "orb", scatter_dimension=1, tiled=True)
    return summed.astype(jnp.bfloat16)


def solution(mesh):
    placed = (
        P("frag", "orb", "aux"),
        P("frag", "orb", "aux", None),
        P("orb", "aux"),
        P(),
        P(),
        P(),
    )
    return jax.shard_map(
        per_device, mesh=mesh, in_specs=placed, out_specs=P("frag", "orb", "aux"), check_vma=False
    )
```

```python
import functools

import jax
import jax.numpy as jnp
from jax import lax
from jax.experimental import pallas as pl
from jax.experimental.pallas import tpu as pltpu
from jax.sharding import PartitionSpec as P

HIGH = lax.Precision.HIGHEST
MESH = pl.DeviceIdType.MESH
BLOCK = 64
SUB = 8
LANES = 128
SIDE = 4

def spread(value, start, j):
    return jnp.take_along_axis(value, start + j, axis=1)

def invert_tiles(pairs):
    lane = lax.broadcasted_iota(jnp.int32, (SUB, LANES), 1)
    sub = lax.broadcasted_iota(jnp.int32, (SUB, LANES), 0)
    inner = lane % BLOCK
    start = lane - inner
    count = BLOCK // SUB
    pivots = [[None] * count for _ in pairs]
    for now in range(count):
        base = now * SUB
        inside = (inner >= base) & (inner < base + SUB)
        for p, slabs in enumerate(pairs):
            rows = [jnp.broadcast_to(slabs[now][t : t + 1], (SUB, LANES)) for t in range(SUB)]
            entry = [[spread(rows[t], start, base + s) for s in range(t + 1)] for t in range(SUB)]
            rows = [jnp.where(inside, jnp.where(inner == base + t, 1.0, 0.0), rows[t]) for t in range(SUB)]
            inverse, factor = [], {}
            for s in range(SUB):
                inverse.append(1.0 / entry[s][s])
                for t in range(s + 1, SUB):
                    factor[t, s] = entry[t][s] * inverse[s]
                for t in range(s + 1, SUB):
                    for u in range(s + 1, t + 1):
                        entry[t][u] = entry[t][u] - factor[t, s] * entry[u][s]
                for t in range(s + 1, SUB):
                    rows[t] = rows[t] - factor[t, s] * rows[s]
            solved, diag = rows[0], entry[0][0]
            for t in range(1, SUB):
                solved = jnp.where(sub == t, rows[t], solved)
                diag = jnp.where(sub == t, entry[t][t], diag)
            slabs[now] = solved
            pivots[p][now] = diag
            weights = [rows[s] * inverse[s] for s in range(SUB)]
            for s in range(SUB - 1, -1, -1):
                for t in range(s + 1, SUB):
                    weights[s] = weights[s] - factor[t, s] * weights[t]
            for later in range(now + 1, count):
                terms = [spread(slabs[later], start, base + s) * weights[s] for s in range(SUB)]
                while len(terms) > 1:
                    terms = [a + b for a, b in zip(terms[::2], terms[1::2])]
                slabs[later] = jnp.where(inside, 0.0, slabs[later]) - terms[0]
    for p, slabs in enumerate(pairs):
        for now in range(count):
            unit = jnp.where(inner < sub + now * SUB, slabs[now], jnp.where(inner == sub + now * SUB, 1.0, 0.0))
            slabs[now] = unit * lax.rsqrt(pivots[p][now])


def inverse_factor(work_ref, tile_ref, frags):
    size = work_ref.shape[1]
    for block in range(size // BLOCK):
        lo, hi = block * BLOCK, (block + 1) * BLOCK
        for i, f in enumerate(frags):
            left = (i % 2) * BLOCK
            tile_ref[i // 2, :, left : left + BLOCK] = work_ref[f, lo:hi, lo:hi]
        pairs = [[tile_ref[p, r : r + SUB, :] for r in range(0, BLOCK, SUB)] for p in range((len(frags) + 1) // 2)]
        invert_tiles(pairs)
        for p, slabs in enumerate(pairs):
            for r, slab in enumerate(slabs):
                tile_ref[p, r * SUB : (r + 1) * SUB, :] = slab
        for i, f in enumerate(frags):
            left = (i % 2) * BLOCK
            inverse = tile_ref[i // 2, :, left : left + BLOCK]
            rows = jnp.dot(inverse, work_ref[f, lo:hi, :], precision=HIGH, preferred_element_type=jnp.float32)
            work_ref[f, lo:hi, :] = rows
            work_ref[f, lo:hi, lo:hi] = inverse
            if hi < size:
                below = jnp.transpose(rows)[hi:, :]
                work_ref[f, hi:, lo:hi] = jnp.zeros((size - hi, BLOCK), jnp.float32)
                work_ref[f, hi:, :] -= jnp.dot(
                    below, work_ref[f, lo:hi, :], precision=HIGH, preferred_element_type=jnp.float32
                )
        yield block


def kernel(
    bath_ref, rows_ref, factor_ref, live_col_ref, live_row_ref, out_ref,
    initial, held, partial, gram, gram_in, tiles, outgoing, incoming,
    send_sem, recv_sem, own_sem, load_sem, gram_sem, value_sem,
):
    frags, nfmax, depth = rows_ref.shape
    nbmax = bath_ref.shape[1]
    size = nfmax + nbmax
    piece = depth // 2
    aux, orb = lax.axis_index("aux"), lax.axis_index("orb")
    up, across = aux // SIDE, aux % SIDE

    def device(coord_up, coord_across):
        return {"aux": coord_up * SIDE + coord_across}

    def turn(value, by):
        return lax.rem(value + by + SIDE, SIDE)

    place = [(across, up), (up, across)]

    def neighbour(half, second, by):
        first, other = place[half]
        if second:
            other = turn(other, by)
        else:
            first = turn(first, by)
        return device(other, first) if half == 0 else device(first, other)

    partner = {"orb": 1 - orb}
    barrier = pltpu.get_barrier_semaphore()
    for half in range(2):
        for by in (1, -1):
            pl.semaphore_signal(barrier, inc=1, device_id=neighbour(half, False, by), device_id_type=MESH)
    pl.semaphore_signal(barrier, inc=1, device_id=partner, device_id_type=MESH)

    units = [("bath", 0), ("bath", 1), ("bath", 2), ("rows", 0), ("rows", 1), ("rows", 2), ("bath", 3), ("rows", 3)]

    def span(unit):
        kind, f = units[unit]
        return f, (0 if kind == "rows" else nfmax), (nfmax if kind == "rows" else nbmax)

    own = []
    for unit, (kind, f) in enumerate(units):
        for half in range(2):
            first, other = place[half]
            source = rows_ref if kind == "rows" else bath_ref
            f, low, count = span(unit)
            column = pl.multiple_of((other * SIDE + first) * piece, piece)
            own.append(
                pltpu.make_async_copy(
                    source.at[f, :, half * piece : (half + 1) * piece],
                    initial.at[half, f, low : low + count, pl.ds(column, piece)],
                    own_sem.at[unit, half],
                )
            )
            own[-1].start()
    loads = []
    for half in range(2):
        for slot in range(SIDE * SIDE):
            other, first = slot // SIDE, slot % SIDE
            source = slot if half == 0 else first * SIDE + other
            loads.append(
                pltpu.make_async_copy(
                    factor_ref.at[source, half], held.at[half, slot], load_sem.at[half, slot]
                )
            )
            loads[-1].start()

    def region(unit, half, second, offset, part):
        f, low, count = span(unit)
        first, other = place[half]
        if part is not None:
            count = count // 2
            low = low + part * count
        if second:
            column, width = turn(other, offset) * SIDE * piece, SIDE * piece
        else:
            column, width = (other * SIDE + turn(first, offset)) * piece, piece
        column = pl.multiple_of(column, piece)
        return initial.at[half, f, low : low + count, pl.ds(column, width)]

    messages = [(0, None, 1), (0, None, -1), (-1, 0, 1), (1, 1, -1)]
    sent = []

    def message(unit, half, second, index):
        offset, part, by = messages[index]
        where = region(unit, half, second, offset, part)
        slot = (4 if second else 0) + index
        return pltpu.make_async_remote_copy(
            src_ref=where,
            dst_ref=where,
            send_sem=send_sem.at[unit, half, slot],
            recv_sem=recv_sem.at[unit, half, slot],
            device_id=neighbour(half, second, by),
            device_id_type=MESH,
        )

    def send(unit, half, second, index):
        copy = message(unit, half, second, index)
        copy.start()
        sent.append(copy)

    def receive(unit, half, second, index):
        offset, part, by = messages[index]
        where = region(unit, half, second, offset - by, part)
        slot = (4 if second else 0) + index
        pltpu.make_async_remote_copy(
            src_ref=where,
            dst_ref=where,
            send_sem=send_sem.at[unit, half, slot],
            recv_sem=recv_sem.at[unit, half, slot],
            device_id=neighbour(half, second, by),
            device_id_type=MESH,
        ).wait_recv()

    passed = set()

    def stage(number, unit):
        if unit >= len(units) or (number, unit) in passed:
            return
        passed.add((number, unit))
        second = number > 2
        for half in range(2):
            if number == 1:
                own[unit * 2 + half].wait()
                send(unit, half, False, 0)
                send(unit, half, False, 1)
            elif number in (2, 4):
                receive(unit, half, second, 0)
                send(unit, half, second, 2)
                receive(unit, half, second, 1)
                send(unit, half, second, 3)
            elif number == 3:
                receive(unit, half, False, 2)
                receive(unit, half, False, 3)
                send(unit, half, True, 0)
                send(unit, half, True, 1)
            else:
                receive(unit, half, True, 2)
                receive(unit, half, True, 3)

    contract = (((1,), (1,)), ((), ()))

    def make_gram(f):
        total = lax.dot_general(initial[0, f], initial[0, f], contract, preferred_element_type=jnp.float32)
        total += lax.dot_general(initial[1, f], initial[1, f], contract, preferred_element_type=jnp.float32)
        gram[f] = total

    def gram_copy(f):
        return pltpu.make_async_remote_copy(
            src_ref=gram.at[f],
            dst_ref=gram_in.at[f],
            send_sem=gram_sem.at[0, f],
            recv_sem=gram_sem.at[1, f],
            device_id=partner,
            device_id_type=MESH,
        )

    width = 256
    tiles_q = partial.shape[2] // width

    def project(f):
        def one(q, carry):
            column = pl.ds(pl.multiple_of(q * width, width), width)
            total = jnp.zeros((size, width), jnp.float32)
            for half in range(2):
                block = held[half, :, :, column].reshape(SIDE * SIDE * piece, width)
                total += jnp.dot(initial[half, f], block, preferred_element_type=jnp.float32)
            partial[f, :, column] = total
            return carry

        lax.fori_loop(0, tiles_q, one, 0)

    row = lax.broadcasted_iota(jnp.int32, (size, size), 0)
    col = lax.broadcasted_iota(jnp.int32, (size, size), 1)

    def prepare(f):
        copy = gram_copy(f)
        copy.wait()
        both = live_col_ref[f] * live_row_ref[f]
        gram_in[f] = jnp.where(both > 0.5, gram[f] + gram_in[f], jnp.where(row == col, 1.0, 0.0))

    def value_copy(f):
        return pltpu.make_async_remote_copy(
            src_ref=outgoing.at[f],
            dst_ref=incoming.at[f],
            send_sem=value_sem.at[0, f],
            recv_sem=value_sem.at[1, f],
            device_id=partner,
            device_id_type=MESH,
        )

    def apply(f):
        both = live_col_ref[f] * live_row_ref[f]
        gram_in[f] = jnp.where((both > 0.5) & (row >= col), gram_in[f], 0.0)
        theirs = gram_in[f, pl.ds(pl.multiple_of((1 - orb) * nfmax, nfmax), nfmax), :]
        mine = gram_in[f, pl.ds(pl.multiple_of(orb * nfmax, nfmax), nfmax), :]
        value = jnp.dot(theirs, partial[f], precision=HIGH, preferred_element_type=jnp.float32)
        outgoing[f] = value.astype(outgoing.dtype)
        value = jnp.dot(mine, partial[f], precision=HIGH, preferred_element_type=jnp.float32)
        value_copy(f).start()
        partial[f, :nfmax, :] = value

    def finish(f):
        value_copy(f).wait()
        out_ref[f] = (partial[f, :nfmax, :] + incoming[f].astype(jnp.float32)).astype(out_ref.dtype)

    pl.semaphore_wait(barrier, 5)
    for unit in range(3):
        stage(1, unit)
    for unit in range(2):
        stage(2, unit)
        stage(3, unit)
    factors = None
    for unit in range(len(units)):
        stage(4, unit)
        stage(1, unit + 3)
        stage(2, unit + 2)
        stage(3, unit + 2)
        stage(5, unit)
        if unit == 3:
            for copy in loads:
                copy.wait()
        kind, f = units[unit]
        if kind == "rows":
            make_gram(f)
            gram_copy(f).start()
            project(f)
        if unit == 5:
            for f in range(3):
                prepare(f)
            factors = inverse_factor(gram_in, tiles, [0, 1, 2])
            next(factors)
            stage(4, 6)
            next(factors)
            stage(4, 7)
        if unit == 6:
            next(factors)
            next(factors)
            for f in range(3):
                apply(f)
    prepare(3)
    for f in range(3):
        finish(f)
    for block in inverse_factor(gram_in, tiles, [3]):
        pass
    apply(3)
    finish(3)
    for copy in sent:
        copy.wait_send()


def fused(bath_rows, rows, factor, live_cols):
    frags, nfmax, depth = rows.shape
    size = live_cols.shape[1]
    columns = factor.shape[1]
    slots, piece = SIDE * SIDE, depth // 2
    sems = pltpu.SemaphoreType.DMA
    half_rows = size // 2
    return pl.pallas_call(
        kernel,
        out_shape=jax.ShapeDtypeStruct((frags, half_rows, columns), jnp.bfloat16),
        in_specs=[pl.BlockSpec(memory_space=pltpu.VMEM)] * 2
        + [pl.BlockSpec(memory_space=pl.ANY)]
        + [pl.BlockSpec(memory_space=pltpu.VMEM)] * 2,
        out_specs=pl.BlockSpec(memory_space=pltpu.VMEM),
        scratch_shapes=[
            pltpu.VMEM((2, frags, size, slots * piece), jnp.bfloat16),
            pltpu.VMEM((2, slots, piece, columns), jnp.bfloat16),
            pltpu.VMEM((frags, size, columns), jnp.float32),
            pltpu.VMEM((frags, size, size), jnp.float32),
            pltpu.VMEM((frags, size, size), jnp.float32),
            pltpu.VMEM((2, BLOCK, LANES), jnp.float32),
            pltpu.VMEM((frags, half_rows, columns), jnp.bfloat16),
            pltpu.VMEM((frags, half_rows, columns), jnp.bfloat16),
            sems((8, 2, 8)),
            sems((8, 2, 8)),
            sems((8, 2)),
            sems((2, slots)),
            sems((2, frags)),
            sems((2, frags)),
        ],
        compiler_params=pltpu.CompilerParams(
            collective_id=0, has_side_effects=True, vmem_limit_bytes=60 * 1024 * 1024
        ),
    )(bath_rows, rows, factor.reshape(slots, 2, piece, columns), live_cols[:, :, None], live_cols[:, None, :])


def per_device(density, bath, factor, frag_index, nfrag, nbath):
    local_rows = density.shape[0]
    block_cols = density.shape[2]
    density_local = density.reshape(local_rows, block_cols)
    group_size = bath.shape[0]
    frag_max = frag_index.shape[1]
    bath_max = bath.shape[3]
    frag_count = frag_index.shape[0]
    row_offset = lax.axis_index("frag") * local_rows
    local_index = frag_index - row_offset
    owned_rows = (local_index >= 0) & (local_index < local_rows)
    picked = jnp.take(density_local, jnp.clip(local_index, 0, local_rows - 1).reshape(-1), axis=0)
    picked = picked.reshape(frag_count, frag_max, block_cols)
    picked = jnp.where(owned_rows[:, :, None], picked, jnp.zeros_like(picked))
    rows = lax.psum_scatter(picked, "frag", scatter_dimension=0, tiled=True)
    first_frag = lax.axis_index("frag") * group_size
    my_nfrag = lax.dynamic_slice_in_dim(nfrag, first_frag, group_size)
    my_nbath = lax.dynamic_slice_in_dim(nbath, first_frag, group_size)
    frag_live = jnp.arange(frag_max, dtype=jnp.int32)[None, :] < my_nfrag[:, None]
    bath_live = jnp.arange(bath_max, dtype=jnp.int32)[None, :] < my_nbath[:, None]
    live_cols = jnp.concatenate([frag_live, bath_live], axis=1).astype(jnp.float32)
    bath_rows = jnp.swapaxes(bath.reshape(group_size, block_cols, bath_max), 1, 2)
    return fused(bath_rows, rows, factor, live_cols)


def solution(mesh):
    placed = (
        P("frag", "orb", "aux"),
        P("frag", "orb", "aux", None),
        P("orb", "aux"),
        P(),
        P(),
        P(),
    )
    return jax.shard_map(
        per_device, mesh=mesh, in_specs=placed, out_specs=P("frag", "orb", "aux"), check_vma=False
    )
```

```python
import functools

import jax
import jax.numpy as jnp
from jax import lax
from jax.experimental import pallas as pl
from jax.experimental.pallas import tpu as pltpu
from jax.sharding import PartitionSpec as P

HIGH = lax.Precision.HIGHEST
MESH = pl.DeviceIdType.MESH
BLOCK = 64
SUB = 8
LANES = 128
SIDE = 4

def spread(value, start, j):
    return jnp.take_along_axis(value, start + j, axis=1)

def invert_tiles(pairs):
    lane = lax.broadcasted_iota(jnp.int32, (SUB, LANES), 1)
    sub = lax.broadcasted_iota(jnp.int32, (SUB, LANES), 0)
    inner = lane % BLOCK
    start = lane - inner
    count = BLOCK // SUB
    pivots = [[None] * count for _ in pairs]
    for now in range(count):
        base = now * SUB
        inside = (inner >= base) & (inner < base + SUB)
        for p, slabs in enumerate(pairs):
            rows = [jnp.broadcast_to(slabs[now][t : t + 1], (SUB, LANES)) for t in range(SUB)]
            entry = [[spread(rows[t], start, base + s) for s in range(t + 1)] for t in range(SUB)]
            rows = [jnp.where(inside, jnp.where(inner == base + t, 1.0, 0.0), rows[t]) for t in range(SUB)]
            inverse, factor = [], {}
            for s in range(SUB):
                inverse.append(1.0 / entry[s][s])
                for t in range(s + 1, SUB):
                    factor[t, s] = entry[t][s] * inverse[s]
                for t in range(s + 1, SUB):
                    for u in range(s + 1, t + 1):
                        entry[t][u] = entry[t][u] - factor[t, s] * entry[u][s]
                for t in range(s + 1, SUB):
                    rows[t] = rows[t] - factor[t, s] * rows[s]
            solved, diag = rows[0], entry[0][0]
            for t in range(1, SUB):
                solved = jnp.where(sub == t, rows[t], solved)
                diag = jnp.where(sub == t, entry[t][t], diag)
            slabs[now] = solved
            pivots[p][now] = diag
            weights = [rows[s] * inverse[s] for s in range(SUB)]
            for s in range(SUB - 1, -1, -1):
                for t in range(s + 1, SUB):
                    weights[s] = weights[s] - factor[t, s] * weights[t]
            for later in range(now + 1, count):
                terms = [spread(slabs[later], start, base + s) * weights[s] for s in range(SUB)]
                while len(terms) > 1:
                    terms = [a + b for a, b in zip(terms[::2], terms[1::2])]
                slabs[later] = jnp.where(inside, 0.0, slabs[later]) - terms[0]
    for p, slabs in enumerate(pairs):
        for now in range(count):
            unit = jnp.where(inner < sub + now * SUB, slabs[now], jnp.where(inner == sub + now * SUB, 1.0, 0.0))
            slabs[now] = unit * lax.rsqrt(pivots[p][now])


def inverse_factor(work_ref, tile_ref, frags):
    size = work_ref.shape[1]
    for block in range(size // BLOCK):
        lo, hi = block * BLOCK, (block + 1) * BLOCK
        for i, f in enumerate(frags):
            left = (i % 2) * BLOCK
            tile_ref[i // 2, :, left : left + BLOCK] = work_ref[f, lo:hi, lo:hi]
        pairs = [[tile_ref[p, r : r + SUB, :] for r in range(0, BLOCK, SUB)] for p in range((len(frags) + 1) // 2)]
        invert_tiles(pairs)
        for p, slabs in enumerate(pairs):
            for r, slab in enumerate(slabs):
                tile_ref[p, r * SUB : (r + 1) * SUB, :] = slab
        for i, f in enumerate(frags):
            left = (i % 2) * BLOCK
            inverse = tile_ref[i // 2, :, left : left + BLOCK]
            rows = jnp.dot(inverse, work_ref[f, lo:hi, :], precision=HIGH, preferred_element_type=jnp.float32)
            work_ref[f, lo:hi, :] = rows
            work_ref[f, lo:hi, lo:hi] = inverse
            if hi < size:
                below = jnp.transpose(rows)[hi:, :]
                work_ref[f, hi:, lo:hi] = jnp.zeros((size - hi, BLOCK), jnp.float32)
                work_ref[f, hi:, :] -= jnp.dot(
                    below, work_ref[f, lo:hi, :], precision=HIGH, preferred_element_type=jnp.float32
                )
        yield block


def kernel(
    bath_ref, density_ref, index_ref, factor_ref, live_col_ref, live_row_ref, out_ref,
    initial, held, partial, gram, gram_in, tiles, outgoing, incoming, density, picked, summed, far,
    send_sem, recv_sem, own_sem, load_sem, gram_sem, value_sem, rows_sem, density_sem,
):
    frags, nbmax, depth = bath_ref.shape
    local_rows = density.shape[0]
    nfmax = picked.shape[3]
    size = nfmax + nbmax
    piece = depth // 2
    aux, orb = lax.axis_index("aux"), lax.axis_index("orb")
    up, across = aux // SIDE, aux % SIDE

    def device(coord_up, coord_across):
        return {"aux": coord_up * SIDE + coord_across}

    def turn(value, by):
        return lax.rem(value + by + SIDE, SIDE)

    place = [(across, up), (up, across)]

    def neighbour(half, second, by):
        first, other = place[half]
        if second:
            other = turn(other, by)
        else:
            first = turn(first, by)
        return device(other, first) if half == 0 else device(first, other)

    partner = {"orb": 1 - orb}
    frag = lax.axis_index("frag")
    high, core = frag // 2, frag % 2
    sibling = {"frag": high * 2 + 1 - core}
    opposite = {"frag": (1 - high) * 2 + core}
    fetch = pltpu.make_async_copy(density_ref, density, density_sem)
    fetch.start()
    barrier = pltpu.get_barrier_semaphore()
    for half in range(2):
        for by in (1, -1):
            pl.semaphore_signal(barrier, inc=1, device_id=neighbour(half, False, by), device_id_type=MESH)
    for other in (partner, sibling, opposite):
        pl.semaphore_signal(barrier, inc=1, device_id=other, device_id_type=MESH)

    units = [("bath", 0), ("bath", 1), ("bath", 2), ("rows", 0), ("rows", 1), ("rows", 2), ("bath", 3), ("rows", 3)]

    def span(unit):
        kind, f = units[unit]
        return f, (0 if kind == "rows" else nfmax), (nfmax if kind == "rows" else nbmax)

    own = {}
    for unit, (kind, f) in enumerate(units):
        for half in range(2):
            if kind == "rows":
                continue
            first, other = place[half]
            f, low, count = span(unit)
            column = pl.multiple_of((other * SIDE + first) * piece, piece)
            own[unit, half] = pltpu.make_async_copy(
                bath_ref.at[f, :, half * piece : (half + 1) * piece],
                initial.at[half, f, low : low + count, pl.ds(column, piece)],
                own_sem.at[unit, half],
            )
            own[unit, half].start()
    loads = []
    for half in range(2):
        for slot in range(SIDE * SIDE):
            other, first = slot // SIDE, slot % SIDE
            source = slot if half == 0 else first * SIDE + other
            loads.append(
                pltpu.make_async_copy(
                    factor_ref.at[source, half], held.at[half, slot], load_sem.at[half, slot]
                )
            )
            loads[-1].start()

    def region(unit, half, second, offset, part):
        f, low, count = span(unit)
        first, other = place[half]
        if part is not None:
            count = count // 2
            low = low + part * count
        if second:
            column, width = turn(other, offset) * SIDE * piece, SIDE * piece
        else:
            column, width = (other * SIDE + turn(first, offset)) * piece, piece
        column = pl.multiple_of(column, piece)
        return initial.at[half, f, low : low + count, pl.ds(column, width)]

    messages = [(0, None, 1), (0, None, -1), (-1, 0, 1), (1, 1, -1)]
    sent = []

    def message(unit, half, second, index):
        offset, part, by = messages[index]
        where = region(unit, half, second, offset, part)
        slot = (4 if second else 0) + index
        return pltpu.make_async_remote_copy(
            src_ref=where,
            dst_ref=where,
            send_sem=send_sem.at[unit, half, slot],
            recv_sem=recv_sem.at[unit, half, slot],
            device_id=neighbour(half, second, by),
            device_id_type=MESH,
        )

    def send(unit, half, second, index):
        copy = message(unit, half, second, index)
        copy.start()
        sent.append(copy)

    def receive(unit, half, second, index):
        offset, part, by = messages[index]
        where = region(unit, half, second, offset - by, part)
        slot = (4 if second else 0) + index
        pltpu.make_async_remote_copy(
            src_ref=where,
            dst_ref=where,
            send_sem=send_sem.at[unit, half, slot],
            recv_sem=recv_sem.at[unit, half, slot],
            device_id=neighbour(half, second, by),
            device_id_type=MESH,
        ).wait_recv()

    passed = set()

    def stage(number, unit):
        if unit >= len(units) or (number, unit) in passed:
            return
        passed.add((number, unit))
        second = number > 2
        for half in range(2):
            if number == 1:
                if (unit, half) in own:
                    own[unit, half].wait()
                send(unit, half, False, 0)
                send(unit, half, False, 1)
            elif number in (2, 4):
                receive(unit, half, second, 0)
                send(unit, half, second, 2)
                receive(unit, half, second, 1)
                send(unit, half, second, 3)
            elif number == 3:
                receive(unit, half, False, 2)
                receive(unit, half, False, 3)
                send(unit, half, True, 0)
                send(unit, half, True, 1)
            else:
                receive(unit, half, True, 2)
                receive(unit, half, True, 3)

    def pick(f):
        step = 8 * LANES
        lane = lax.broadcasted_iota(jnp.int32, (index_ref.shape[1], LANES), 1)

        def one(block, total):
            hot = [
                jnp.where(index_ref[f] == lane + (block * step + part * LANES), 1.0, 0.0).astype(jnp.bfloat16)
                for part in range(8)
            ]
            rows = density[pl.ds(pl.multiple_of(block * step, step), step), :]
            return total + jnp.dot(jnp.concatenate(hot, axis=1), rows, preferred_element_type=jnp.float32)

        total = lax.fori_loop(0, local_rows // step, one, jnp.zeros((index_ref.shape[1], depth), jnp.float32))
        picked[f] = total.astype(picked.dtype).reshape(picked.shape[1:])

    def sibling_copy(f):
        return pltpu.make_async_remote_copy(
            src_ref=picked.at[f, 1 - core],
            dst_ref=summed.at[f],
            send_sem=rows_sem.at[0, f],
            recv_sem=rows_sem.at[1, f],
            device_id=sibling,
            device_id_type=MESH,
        )

    def far_copy(f):
        return pltpu.make_async_remote_copy(
            src_ref=summed.at[f, 1 - high],
            dst_ref=far.at[f],
            send_sem=rows_sem.at[2, f],
            recv_sem=rows_sem.at[3, f],
            device_id=opposite,
            device_id_type=MESH,
        )

    def send_picked(f):
        sibling_copy(f).start()

    def add_sibling(f):
        sibling_copy(f).wait()
        summed[f] = summed[f] + picked[f, core]

    def send_far(f):
        far_copy(f).start()

    def take_rows(f):
        far_copy(f).wait()
        value = summed[f, high] + far[f]
        for half in range(2):
            first, other = place[half]
            column = pl.multiple_of((other * SIDE + first) * piece, piece)
            initial[half, f, :nfmax, pl.ds(column, piece)] = value[:, half * piece : (half + 1) * piece]

    contract = (((1,), (1,)), ((), ()))

    def make_gram(f):
        total = lax.dot_general(initial[0, f], initial[0, f], contract, preferred_element_type=jnp.float32)
        total += lax.dot_general(initial[1, f], initial[1, f], contract, preferred_element_type=jnp.float32)
        gram[f] = total

    def gram_copy(f):
        return pltpu.make_async_remote_copy(
            src_ref=gram.at[f],
            dst_ref=gram_in.at[f],
            send_sem=gram_sem.at[0, f],
            recv_sem=gram_sem.at[1, f],
            device_id=partner,
            device_id_type=MESH,
        )

    width = 256
    tiles_q = partial.shape[2] // width

    def project(f):
        def one(q, carry):
            column = pl.ds(pl.multiple_of(q * width, width), width)
            total = jnp.zeros((size, width), jnp.float32)
            for half in range(2):
                block = held[half, :, :, column].reshape(SIDE * SIDE * piece, width)
                total += jnp.dot(initial[half, f], block, preferred_element_type=jnp.float32)
            partial[f, :, column] = total
            return carry

        lax.fori_loop(0, tiles_q, one, 0)

    row = lax.broadcasted_iota(jnp.int32, (size, size), 0)
    col = lax.broadcasted_iota(jnp.int32, (size, size), 1)

    def prepare(f):
        copy = gram_copy(f)
        copy.wait()
        both = live_col_ref[f] * live_row_ref[f]
        gram_in[f] = jnp.where(both > 0.5, gram[f] + gram_in[f], jnp.where(row == col, 1.0, 0.0))

    def value_copy(f):
        return pltpu.make_async_remote_copy(
            src_ref=outgoing.at[f],
            dst_ref=incoming.at[f],
            send_sem=value_sem.at[0, f],
            recv_sem=value_sem.at[1, f],
            device_id=partner,
            device_id_type=MESH,
        )

    def apply(f):
        both = live_col_ref[f] * live_row_ref[f]
        gram_in[f] = jnp.where((both > 0.5) & (row >= col), gram_in[f], 0.0)
        theirs = gram_in[f, pl.ds(pl.multiple_of((1 - orb) * nfmax, nfmax), nfmax), :]
        mine = gram_in[f, pl.ds(pl.multiple_of(orb * nfmax, nfmax), nfmax), :]
        value = jnp.dot(theirs, partial[f], precision=HIGH, preferred_element_type=jnp.float32)
        outgoing[f] = value.astype(outgoing.dtype)
        value = jnp.dot(mine, partial[f], precision=HIGH, preferred_element_type=jnp.float32)
        value_copy(f).start()
        partial[f, :nfmax, :] = value

    def finish(f):
        value_copy(f).wait()
        out_ref[f] = (partial[f, :nfmax, :] + incoming[f].astype(jnp.float32)).astype(out_ref.dtype)

    pl.semaphore_wait(barrier, 7)
    for unit in range(3):
        stage(1, unit)
    fetch.wait()
    pick(0)
    stage(2, 0)
    stage(3, 0)
    send_picked(0)
    pick(1)
    stage(2, 1)
    stage(3, 1)
    send_picked(1)
    add_sibling(0)
    stage(4, 0)
    pick(2)
    send_far(0)
    send_picked(2)
    stage(2, 2)
    stage(3, 2)
    add_sibling(1)
    stage(5, 0)
    pick(3)
    send_far(1)
    send_picked(3)
    add_sibling(2)
    take_rows(0)
    stage(4, 1)
    send_far(2)
    stage(1, 3)
    add_sibling(3)
    factors = None
    for unit in range(1, len(units)):
        stage(4, unit)
        if unit == 1:
            send_far(3)
        if unit + 3 < len(units) and units[unit + 3][0] == "rows":
            take_rows(units[unit + 3][1])
        stage(2, unit + 2)
        stage(3, unit + 2)
        stage(1, unit + 3)
        stage(5, unit)
        if unit == 3:
            for copy in loads:
                copy.wait()
        kind, f = units[unit]
        if kind == "rows":
            make_gram(f)
            gram_copy(f).start()
            project(f)
        if unit == 5:
            for f in range(3):
                prepare(f)
            factors = inverse_factor(gram_in, tiles, [0, 1, 2])
            next(factors)
            stage(4, 6)
            next(factors)
            stage(4, 7)
        if unit == 6:
            next(factors)
            next(factors)
            for f in range(3):
                apply(f)
    prepare(3)
    for f in range(3):
        finish(f)
    for block in inverse_factor(gram_in, tiles, [3]):
        pass
    apply(3)
    finish(3)
    for copy in sent:
        copy.wait_send()


def fused(bath_rows, density, index, factor, live_cols):
    frags, nbmax, depth = bath_rows.shape
    local_rows = density.shape[0]
    groups = index.shape[1] // (live_cols.shape[1] - nbmax)
    size = live_cols.shape[1]
    columns = factor.shape[1]
    slots, piece = SIDE * SIDE, depth // 2
    sems = pltpu.SemaphoreType.DMA
    half_rows = size // 2
    return pl.pallas_call(
        kernel,
        out_shape=jax.ShapeDtypeStruct((frags, half_rows, columns), jnp.bfloat16),
        in_specs=[
            pl.BlockSpec(memory_space=kind)
            for kind in (pltpu.VMEM, pl.ANY, pltpu.VMEM, pl.ANY, pltpu.VMEM, pltpu.VMEM)
        ],
        out_specs=pl.BlockSpec(memory_space=pltpu.VMEM),
        scratch_shapes=[
            pltpu.VMEM((2, frags, size, slots * piece), jnp.bfloat16),
            pltpu.VMEM((2, slots, piece, columns), jnp.bfloat16),
            pltpu.VMEM((frags, size, columns), jnp.float32),
            pltpu.VMEM((frags, size, size), jnp.float32),
            pltpu.VMEM((frags, size, size), jnp.float32),
            pltpu.VMEM((2, BLOCK, LANES), jnp.float32),
            pltpu.VMEM((frags, half_rows, columns), jnp.bfloat16),
            pltpu.VMEM((frags, half_rows, columns), jnp.bfloat16),
            pltpu.VMEM((local_rows, depth), jnp.bfloat16),
            pltpu.VMEM((frags, 2, groups // 2, size - nbmax, depth), jnp.bfloat16),
            pltpu.VMEM((frags, groups // 2, size - nbmax, depth), jnp.bfloat16),
            pltpu.VMEM((frags, size - nbmax, depth), jnp.bfloat16),
            sems((8, 2, 8)),
            sems((8, 2, 8)),
            sems((8, 2)),
            sems((2, slots)),
            sems((2, frags)),
            sems((2, frags)),
            sems((4, frags)),
            sems(()),
        ],
        compiler_params=pltpu.CompilerParams(
            collective_id=0, has_side_effects=True, vmem_limit_bytes=60 * 1024 * 1024
        ),
    )(bath_rows, density, index, factor.reshape(slots, 2, piece, columns), live_cols[:, :, None], live_cols[:, None, :])


def per_device(density, bath, factor, frag_index, nfrag, nbath):
    local_rows = density.shape[0]
    block_cols = density.shape[2]
    density_local = density.reshape(local_rows, block_cols)
    group_size = bath.shape[0]
    frag_max = frag_index.shape[1]
    bath_max = bath.shape[3]
    frag_count = frag_index.shape[0]
    local_index = frag_index - lax.axis_index("frag") * local_rows
    local_index = local_index.reshape(2, 2, group_size, frag_max).transpose(2, 1, 0, 3)
    local_index = local_index.reshape(group_size, frag_count // group_size * frag_max, 1)
    local_index = jnp.broadcast_to(local_index, local_index.shape[:2] + (LANES,))
    first_frag = lax.axis_index("frag") * group_size
    my_nfrag = lax.dynamic_slice_in_dim(nfrag, first_frag, group_size)
    my_nbath = lax.dynamic_slice_in_dim(nbath, first_frag, group_size)
    frag_live = jnp.arange(frag_max, dtype=jnp.int32)[None, :] < my_nfrag[:, None]
    bath_live = jnp.arange(bath_max, dtype=jnp.int32)[None, :] < my_nbath[:, None]
    live_cols = jnp.concatenate([frag_live, bath_live], axis=1).astype(jnp.float32)
    bath_rows = jnp.swapaxes(bath.reshape(group_size, block_cols, bath_max), 1, 2)
    return fused(bath_rows, density_local, local_index, factor, live_cols)


def solution(mesh):
    placed = (
        P("frag", "orb", "aux"),
        P("frag", "orb", "aux", None),
        P("orb", "aux"),
        P(),
        P(),
        P(),
    )
    return jax.shard_map(
        per_device, mesh=mesh, in_specs=placed, out_specs=P("frag", "orb", "aux"), check_vma=False
    )
```

```python
import functools

import jax
import jax.numpy as jnp
from jax import lax
from jax.experimental import pallas as pl
from jax.experimental.pallas import tpu as pltpu
from jax.sharding import PartitionSpec as P

HIGH = lax.Precision.HIGHEST
MESH = pl.DeviceIdType.MESH
BLOCK = 64
SUB = 8
LANES = 128
SIDE = 4

def spread(value, start, j):
    return jnp.take_along_axis(value, start + j, axis=1)

def invert_tiles(pairs):
    lane = lax.broadcasted_iota(jnp.int32, (SUB, LANES), 1)
    sub = lax.broadcasted_iota(jnp.int32, (SUB, LANES), 0)
    inner = lane % BLOCK
    start = lane - inner
    count = BLOCK // SUB
    pivots = [[None] * count for _ in pairs]
    for now in range(count):
        base = now * SUB
        inside = (inner >= base) & (inner < base + SUB)
        for p, slabs in enumerate(pairs):
            rows = [jnp.broadcast_to(slabs[now][t : t + 1], (SUB, LANES)) for t in range(SUB)]
            entry = [[spread(rows[t], start, base + s) for s in range(t + 1)] for t in range(SUB)]
            rows = [jnp.where(inside, jnp.where(inner == base + t, 1.0, 0.0), rows[t]) for t in range(SUB)]
            inverse, factor = [], {}
            for s in range(SUB):
                inverse.append(1.0 / entry[s][s])
                for t in range(s + 1, SUB):
                    factor[t, s] = entry[t][s] * inverse[s]
                for t in range(s + 1, SUB):
                    for u in range(s + 1, t + 1):
                        entry[t][u] = entry[t][u] - factor[t, s] * entry[u][s]
                for t in range(s + 1, SUB):
                    rows[t] = rows[t] - factor[t, s] * rows[s]
            solved, diag = rows[0], entry[0][0]
            for t in range(1, SUB):
                solved = jnp.where(sub == t, rows[t], solved)
                diag = jnp.where(sub == t, entry[t][t], diag)
            slabs[now] = solved
            pivots[p][now] = diag
            weights = [rows[s] * inverse[s] for s in range(SUB)]
            for s in range(SUB - 1, -1, -1):
                for t in range(s + 1, SUB):
                    weights[s] = weights[s] - factor[t, s] * weights[t]
            for later in range(now + 1, count):
                terms = [spread(slabs[later], start, base + s) * weights[s] for s in range(SUB)]
                while len(terms) > 1:
                    terms = [a + b for a, b in zip(terms[::2], terms[1::2])]
                slabs[later] = jnp.where(inside, 0.0, slabs[later]) - terms[0]
    for p, slabs in enumerate(pairs):
        for now in range(count):
            unit = jnp.where(inner < sub + now * SUB, slabs[now], jnp.where(inner == sub + now * SUB, 1.0, 0.0))
            slabs[now] = unit * lax.rsqrt(pivots[p][now])


def inverse_factor(work_ref, tile_ref, frags):
    size = work_ref.shape[1]
    for block in range(size // BLOCK):
        lo, hi = block * BLOCK, (block + 1) * BLOCK
        for i, f in enumerate(frags):
            left = (i % 2) * BLOCK
            tile_ref[i // 2, :, left : left + BLOCK] = work_ref[f, lo:hi, lo:hi]
        pairs = [[tile_ref[p, r : r + SUB, :] for r in range(0, BLOCK, SUB)] for p in range((len(frags) + 1) // 2)]
        invert_tiles(pairs)
        for p, slabs in enumerate(pairs):
            for r, slab in enumerate(slabs):
                tile_ref[p, r * SUB : (r + 1) * SUB, :] = slab
        for i, f in enumerate(frags):
            left = (i % 2) * BLOCK
            inverse = tile_ref[i // 2, :, left : left + BLOCK]
            rows = jnp.dot(inverse, work_ref[f, lo:hi, :], precision=HIGH, preferred_element_type=jnp.float32)
            work_ref[f, lo:hi, :] = rows
            work_ref[f, lo:hi, lo:hi] = inverse
            if hi < size:
                below = jnp.transpose(rows)[hi:, :]
                work_ref[f, hi:, lo:hi] = jnp.zeros((size - hi, BLOCK), jnp.float32)
                work_ref[f, hi:, :] -= jnp.dot(
                    below, work_ref[f, lo:hi, :], precision=HIGH, preferred_element_type=jnp.float32
                )
        yield block


def kernel(
    nfrag_ref, nbath_ref, bath_ref, density_ref, index_ref, factor_ref, out_ref,
    initial, held, partial, gram, gram_in, tiles, outgoing, incoming, density, picked, summed, far, shares, index,
    send_sem, recv_sem, load_sem, gram_sem, value_sem, rows_sem, density_sem, share_sem,
):
    frags, depth, nbmax = bath_ref.shape
    local_rows = density.shape[0]
    nfmax = picked.shape[3]
    size = nfmax + nbmax
    piece = depth // 2
    aux, orb = lax.axis_index("aux"), lax.axis_index("orb")
    up, across = aux // SIDE, aux % SIDE

    def device(coord_up, coord_across):
        return {"aux": coord_up * SIDE + coord_across}

    def turn(value, by):
        return lax.rem(value + by + SIDE, SIDE)

    place = [(across, up), (up, across)]

    def neighbour(half, second, by):
        first, other = place[half]
        if second:
            other = turn(other, by)
        else:
            first = turn(first, by)
        return device(other, first) if half == 0 else device(first, other)

    frag = lax.axis_index("frag")
    high, core = frag // 2, frag % 2
    sibling = {"frag": high * 2 + 1 - core}
    opposite = {"frag": (1 - high) * 2 + core}
    ranks = SIDE * SIDE

    def rank(by):
        return lax.rem(aux + by + ranks, ranks)

    barrier = pltpu.get_barrier_semaphore()
    greeted = [{"aux": rank(by)} for by in range(1, ranks)] + [{"orb": 1 - orb}, sibling, opposite]
    for other in greeted:
        pl.semaphore_signal(barrier, inc=1, device_id=other, device_id_type=MESH)
    partner = {"orb": 1 - orb}
    fetch = pltpu.make_async_copy(density_ref, density, density_sem)
    fetch.start()

    units = [("bath", 0), ("bath", 1), ("rows", 0), ("rows", 1), ("bath", 2), ("rows", 2), ("bath", 3), ("rows", 3)]

    def span(unit):
        kind, f = units[unit]
        return f, (0 if kind == "rows" else nfmax), (nfmax if kind == "rows" else nbmax)

    def put(half, f, low, value):
        first, other = place[half]
        column = pl.multiple_of((other * SIDE + first) * piece, piece)
        initial[half, f, low : low + value.shape[0], pl.ds(column, piece)] = value

    def put_bath(f):
        for half in range(2):
            put(half, f, nfmax, jnp.transpose(bath_ref[f, half * piece : (half + 1) * piece, :]))

    column_index = jnp.transpose(index_ref[...].astype(jnp.float32))
    for f in range(frags):
        for place_of, group in enumerate((0, 2, 1, 3)):
            low = place_of * nfmax
            value = column_index[:, group * frags + f : group * frags + f + 1]
            index[f, low : low + nfmax, :] = jnp.broadcast_to(value, (nfmax, LANES)).astype(jnp.int32)
    for f in range(frags):
        put_bath(f)

    loads = []
    for half in range(2):
        for slot in range(SIDE * SIDE):
            other, first = slot // SIDE, slot % SIDE
            source = slot if half == 0 else first * SIDE + other
            loads.append(
                pltpu.make_async_copy(
                    factor_ref.at[source, half], held.at[half, slot], load_sem.at[half, slot]
                )
            )
            loads[-1].start()

    def region(unit, half, second, offset, part):
        f, low, count = span(unit)
        first, other = place[half]
        if part is not None:
            count = count // 2
            low = low + part * count
        if second:
            column, width = turn(other, offset) * SIDE * piece, SIDE * piece
        else:
            column, width = (other * SIDE + turn(first, offset)) * piece, piece
        column = pl.multiple_of(column, piece)
        return initial.at[half, f, low : low + count, pl.ds(column, width)]

    messages = [(0, None, 1), (0, None, -1), (-1, 0, 1), (1, 1, -1)]
    sent = []

    def message(unit, half, second, index):
        offset, part, by = messages[index]
        where = region(unit, half, second, offset, part)
        slot = (4 if second else 0) + index
        return pltpu.make_async_remote_copy(
            src_ref=where,
            dst_ref=where,
            send_sem=send_sem.at[unit, half, slot],
            recv_sem=recv_sem.at[unit, half, slot],
            device_id=neighbour(half, second, by),
            device_id_type=MESH,
        )

    def send(unit, half, second, index):
        copy = message(unit, half, second, index)
        copy.start()
        sent.append(copy)

    def receive(unit, half, second, index):
        offset, part, by = messages[index]
        where = region(unit, half, second, offset - by, part)
        slot = (4 if second else 0) + index
        pltpu.make_async_remote_copy(
            src_ref=where,
            dst_ref=where,
            send_sem=send_sem.at[unit, half, slot],
            recv_sem=recv_sem.at[unit, half, slot],
            device_id=neighbour(half, second, by),
            device_id_type=MESH,
        ).wait_recv()

    passed = set()

    def stage(number, unit):
        if unit >= len(units) or (number, unit) in passed:
            return
        passed.add((number, unit))
        second = number > 2
        for half in range(2):
            if number == 1:
                send(unit, half, False, 0)
                send(unit, half, False, 1)
            elif number in (2, 4):
                receive(unit, half, second, 0)
                send(unit, half, second, 2)
                receive(unit, half, second, 1)
                send(unit, half, second, 3)
            elif number == 3:
                receive(unit, half, False, 2)
                receive(unit, half, False, 3)
                send(unit, half, True, 0)
                send(unit, half, True, 1)
            else:
                receive(unit, half, True, 2)
                receive(unit, half, True, 3)

    def pick(f):
        step = 8 * LANES
        lane = lax.broadcasted_iota(jnp.int32, (index.shape[1], LANES), 1) + frag * local_rows
        total = jnp.zeros((index.shape[1], depth), jnp.float32)
        for block in range(local_rows // step):
            hot = [
                jnp.where(index[f] == lane + (block * step + part * LANES), 1.0, 0.0).astype(jnp.bfloat16)
                for part in range(8)
            ]
            rows = density[block * step : (block + 1) * step, :]
            total += jnp.dot(jnp.concatenate(hot, axis=1), rows, preferred_element_type=jnp.float32)
        picked[f] = total.astype(picked.dtype).reshape(picked.shape[1:])

    def sibling_copy(f):
        return pltpu.make_async_remote_copy(
            src_ref=picked.at[f, 1 - core],
            dst_ref=summed.at[f],
            send_sem=rows_sem.at[0, f],
            recv_sem=rows_sem.at[1, f],
            device_id=sibling,
            device_id_type=MESH,
        )

    def far_copy(f):
        return pltpu.make_async_remote_copy(
            src_ref=summed.at[f, 1 - high],
            dst_ref=far.at[f],
            send_sem=rows_sem.at[2, f],
            recv_sem=rows_sem.at[3, f],
            device_id=opposite,
            device_id_type=MESH,
        )

    def send_picked(f):
        sibling_copy(f).start()

    def add_sibling(f):
        sibling_copy(f).wait()
        summed[f] = summed[f] + picked[f, core]

    def send_far(f):
        far_copy(f).start()

    def take_rows(f):
        far_copy(f).wait()
        value = summed[f, high] + far[f]
        for half in range(2):
            put(half, f, 0, value[:, half * piece : (half + 1) * piece])

    contract = (((1,), (1,)), ((), ()))

    def make_gram(f):
        total = lax.dot_general(initial[0, f], initial[0, f], contract, preferred_element_type=jnp.float32)
        total += lax.dot_general(initial[1, f], initial[1, f], contract, preferred_element_type=jnp.float32)
        gram[f] = total

    def gram_copy(f):
        return pltpu.make_async_remote_copy(
            src_ref=gram.at[f],
            dst_ref=gram_in.at[f],
            send_sem=gram_sem.at[0, f],
            recv_sem=gram_sem.at[1, f],
            device_id=partner,
            device_id_type=MESH,
        )

    share = size // ranks
    early = frags - 1

    def my_share():
        return pl.ds(pl.multiple_of(aux * share, share), share)

    def early_gram():
        total = jnp.zeros((size, size), jnp.float32)
        for half in range(2):
            first, other = place[half]
            column = pl.multiple_of((other * SIDE + first) * piece, piece)
            block = initial[half, early, :, pl.ds(column, piece)]
            total += lax.dot_general(block, block, contract, preferred_element_type=jnp.float32)
        gram[early] = total

    def share_copy(by):
        rows_of = pl.ds(pl.multiple_of(rank(by) * share, share), share)
        return pltpu.make_async_remote_copy(
            src_ref=gram.at[early, rows_of, :],
            dst_ref=shares.at[by],
            send_sem=share_sem.at[0, by],
            recv_sem=share_sem.at[1, by],
            device_id={"aux": rank(by)},
            device_id_type=MESH,
        )

    def share_swap():
        return pltpu.make_async_remote_copy(
            src_ref=shares.at[0],
            dst_ref=shares.at[ranks],
            send_sem=share_sem.at[0, 0],
            recv_sem=share_sem.at[1, 0],
            device_id=partner,
            device_id_type=MESH,
        )

    def total_copy(by, source):
        rows_of = pl.ds(pl.multiple_of(rank(source) * share, share), share)
        return pltpu.make_async_remote_copy(
            src_ref=gram_in.at[early, rows_of, :],
            dst_ref=gram_in.at[early, rows_of, :],
            send_sem=share_sem.at[2, by],
            recv_sem=share_sem.at[3, by],
            device_id={"aux": rank(by)},
            device_id_type=MESH,
        )

    def early_send():
        for by in range(1, ranks):
            share_copy(by).start()

    def early_sum():
        for by in range(1, ranks):
            share_copy(by).wait()
        total = gram[early, my_share(), :]
        for by in range(1, ranks):
            total = total + shares[by]
        shares[0] = total

    def early_swap():
        share_swap().start()

    def early_total():
        share_swap().wait()
        gram_in[early, my_share(), :] = shares[0] + shares[ranks]

    def early_spread():
        for by in range(1, ranks):
            total_copy(by, 0).start()

    def early_take():
        for by in range(1, ranks):
            total_copy(by, 0).wait_send()
            total_copy(by, -by).wait_recv()

    width = 512
    tiles_q = partial.shape[2] // width

    def project(f, low=0, high_row=size, offsets=None):
        count = high_row - low

        def one(q, carry):
            column = pl.ds(pl.multiple_of(q * width, width), width)
            total = jnp.zeros((count, width), jnp.float32)
            for half in range(2):
                if offsets is None:
                    block = held[half, :, :, column].reshape(SIDE * SIDE * piece, width)
                    total += jnp.dot(initial[half, f, low:high_row], block, preferred_element_type=jnp.float32)
                    continue
                for offset in offsets:
                    start = turn(place[half][1], offset) * SIDE
                    block = held[half, pl.ds(start, SIDE), :, column].reshape(SIDE * piece, width)
                    columns = pl.ds(pl.multiple_of(start * piece, piece), SIDE * piece)
                    total += jnp.dot(initial[half, f, low:high_row, columns], block, preferred_element_type=jnp.float32)
            if offsets is not None and offsets[0] != 0:
                total += partial[f, low:high_row, column]
            partial[f, low:high_row, column] = total
            return carry

        lax.fori_loop(0, tiles_q, one, 0)

    row = lax.broadcasted_iota(jnp.int32, (size, size), 0)
    col = lax.broadcasted_iota(jnp.int32, (size, size), 1)

    def both_live(f):
        fragment = frag * frags + f
        used, used_bath = nfrag_ref[fragment], nbath_ref[fragment] + nfmax
        live_row = (row < used) | ((row >= nfmax) & (row < used_bath))
        live_col = (col < used) | ((col >= nfmax) & (col < used_bath))
        return live_row & live_col

    def prepare(f):
        total = gram_in[f]
        if f != early:
            gram_copy(f).wait()
            total = gram[f] + gram_in[f]
        gram_in[f] = jnp.where(both_live(f), total, jnp.where(row == col, 1.0, 0.0))

    def value_copy(f):
        return pltpu.make_async_remote_copy(
            src_ref=outgoing.at[f],
            dst_ref=incoming.at[f],
            send_sem=value_sem.at[0, f],
            recv_sem=value_sem.at[1, f],
            device_id=partner,
            device_id_type=MESH,
        )

    def mask(f):
        gram_in[f] = jnp.where(both_live(f) & (row >= col), gram_in[f], 0.0)

    def apply(f):
        theirs = gram_in[f, pl.ds(pl.multiple_of((1 - orb) * nfmax, nfmax), nfmax), :]
        mine = gram_in[f, pl.ds(pl.multiple_of(orb * nfmax, nfmax), nfmax), :]
        value = jnp.dot(theirs, partial[f], precision=HIGH, preferred_element_type=jnp.float32)
        outgoing[f] = value.astype(outgoing.dtype)
        value = jnp.dot(mine, partial[f], precision=HIGH, preferred_element_type=jnp.float32)
        value_copy(f).start()
        partial[f, :nfmax, :] = value

    def finish(f):
        value_copy(f).wait()
        out_ref[f] = (partial[f, :nfmax, :] + incoming[f].astype(jnp.float32)).astype(out_ref.dtype)

    pl.semaphore_wait(barrier, len(greeted))
    stage(1, 0)
    stage(1, 1)
    fetch.wait()
    pick(0)
    stage(2, 0)
    stage(3, 0)
    send_picked(0)
    pick(1)
    stage(2, 1)
    stage(3, 1)
    add_sibling(0)
    send_picked(1)
    stage(1, 4)
    send_far(0)
    pick(2)
    stage(4, 0)
    add_sibling(1)
    send_picked(2)
    take_rows(0)
    send_far(1)
    stage(1, 2)
    pick(3)
    take_rows(1)
    send_picked(3)
    add_sibling(2)
    stage(1, 3)
    stage(2, 2)
    stage(3, 2)
    send_far(2)
    add_sibling(3)
    stage(5, 0)
    send_far(3)
    for copy in loads:
        copy.wait()
    project(0, nfmax, size)
    stage(4, 1)
    stage(2, 3)
    stage(3, 3)
    take_rows(2)
    take_rows(3)
    early_gram()
    stage(5, 1)
    early_send()
    project(1, nfmax, size)
    stage(4, 2)
    stage(2, 4)
    stage(3, 4)
    stage(1, 5)
    early_sum()
    stage(5, 2)
    early_swap()
    make_gram(0)
    project(0, 0, nfmax)
    gram_copy(0).start()
    stage(4, 3)
    early_total()
    stage(1, 6)
    stage(2, 5)
    stage(3, 5)
    early_spread()
    stage(5, 3)
    make_gram(1)
    project(1, 0, nfmax)
    gram_copy(1).start()
    stage(4, 4)
    stage(1, 7)
    stage(2, 6)
    stage(3, 6)
    prepare(0)
    early_take()
    prepare(1)
    steps = inverse_factor(gram_in, tiles, [0,1])
    next(steps)
    stage(5, 4)
    next(steps)
    stage(4, 5)
    stage(2, 7)
    stage(3, 7)
    project(2, nfmax, size)
    next(steps)
    stage(5, 5)
    make_gram(2)
    next(steps)
    gram_copy(2).start()
    stage(4, 6)
    mask(0)
    mask(1)
    apply(0)
    apply(1)
    project(2, 0, nfmax)
    prepare(2)
    prepare(3)
    stage(5, 6)
    steps = inverse_factor(gram_in, tiles, [2,3])
    next(steps)
    stage(4, 7)
    next(steps)
    project(3, nfmax, size)
    next(steps)
    project(3, 0, nfmax, (0,))
    project(3, 0, nfmax, (-1,1))
    next(steps)
    mask(2)
    mask(3)
    apply(2)
    stage(5, 7)
    project(3, 0, nfmax, (2,))
    apply(3)
    finish(0)
    finish(1)
    finish(2)
    finish(3)
    for copy in sent:
        copy.wait_send()


def fused(nfrag, nbath, bath, density, index, factor):
    frags, depth, nbmax = bath.shape
    local_rows = density.shape[0]
    total_frags, nfmax = index.shape
    groups = total_frags // frags
    size = nfmax + nbmax
    columns = factor.shape[1]
    ranks, piece = SIDE * SIDE, depth // 2
    sems = pltpu.SemaphoreType.DMA
    half_rows = size // 2
    vmem = pltpu.VMEM
    return pl.pallas_call(
        kernel,
        out_shape=jax.ShapeDtypeStruct((frags, half_rows, columns), jnp.bfloat16),
        in_specs=[
            pl.BlockSpec(memory_space=kind)
            for kind in (pltpu.SMEM, pltpu.SMEM, vmem, pl.ANY, vmem, pl.ANY)
        ],
        out_specs=pl.BlockSpec(memory_space=vmem),
        scratch_shapes=[
            vmem((2, frags, size, ranks * piece), jnp.bfloat16),
            vmem((2, ranks, piece, columns), jnp.bfloat16),
            vmem((frags, size, columns), jnp.float32),
            vmem((frags, size, size), jnp.float32),
            vmem((frags, size, size), jnp.float32),
            vmem((2, BLOCK, LANES), jnp.float32),
            vmem((frags, half_rows, columns), jnp.bfloat16),
            vmem((frags, half_rows, columns), jnp.bfloat16),
            vmem((local_rows, depth), jnp.bfloat16),
            vmem((frags, 2, groups // 2, nfmax, depth), jnp.bfloat16),
            vmem((frags, groups // 2, nfmax, depth), jnp.bfloat16),
            vmem((frags, nfmax, depth), jnp.bfloat16),
            vmem((ranks + 1, size // ranks, size), jnp.float32),
            vmem((frags, groups * nfmax, LANES), jnp.int32),
            sems((2 * frags, 2, 8)),
            sems((2 * frags, 2, 8)),
            sems((2, ranks)),
            sems((2, frags)),
            sems((2, frags)),
            sems((4, frags)),
            sems(()),
            sems((4, ranks)),
        ],
        compiler_params=pltpu.CompilerParams(
            collective_id=0, has_side_effects=True, vmem_limit_bytes=63 * 1024 * 1024
        ),
    )(nfrag, nbath, bath, density, index, factor.reshape(ranks, 2, piece, columns))


def per_device(density, bath, factor, frag_index, nfrag, nbath):
    local_rows, _, depth = density.shape
    frags, _, _, nbmax = bath.shape
    return fused(
        nfrag, nbath, bath.reshape(frags, depth, nbmax), density.reshape(local_rows, depth), frag_index, factor
    )


def solution(mesh):
    placed = (
        P("frag", "orb", "aux"),
        P("frag", "orb", "aux", None),
        P("orb", "aux"),
        P(),
        P(),
        P(),
    )
    return jax.shard_map(
        per_device, mesh=mesh, in_specs=placed, out_specs=P("frag", "orb", "aux"), check_vma=False
    )
```

```python
import functools

import jax
import jax.numpy as jnp
from jax import lax
from jax.experimental import pallas as pl
from jax.experimental.pallas import tpu as pltpu
from jax.sharding import PartitionSpec as P

HIGH = lax.Precision.HIGHEST
MESH = pl.DeviceIdType.MESH
BLOCK = 64
SUB = 8
LANES = 128
SIDE = 4

def spread(value, start, j):
    return jnp.take_along_axis(value, start + j, axis=1)

def invert_tiles(pairs):
    lane = lax.broadcasted_iota(jnp.int32, (SUB, LANES), 1)
    sub = lax.broadcasted_iota(jnp.int32, (SUB, LANES), 0)
    inner = lane % BLOCK
    start = lane - inner
    count = BLOCK // SUB
    pivots = [[None] * count for _ in pairs]
    for now in range(count):
        base = now * SUB
        inside = (inner >= base) & (inner < base + SUB)
        for p, slabs in enumerate(pairs):
            rows = [jnp.broadcast_to(slabs[now][t : t + 1], (SUB, LANES)) for t in range(SUB)]
            entry = [[spread(rows[t], start, base + s) for s in range(t + 1)] for t in range(SUB)]
            rows = [jnp.where(inside, jnp.where(inner == base + t, 1.0, 0.0), rows[t]) for t in range(SUB)]
            inverse, factor = [], {}
            for s in range(SUB):
                inverse.append(1.0 / entry[s][s])
                for t in range(s + 1, SUB):
                    factor[t, s] = entry[t][s] * inverse[s]
                for t in range(s + 1, SUB):
                    for u in range(s + 1, t + 1):
                        entry[t][u] = entry[t][u] - factor[t, s] * entry[u][s]
                for t in range(s + 1, SUB):
                    rows[t] = rows[t] - factor[t, s] * rows[s]
            solved, diag = rows[0], entry[0][0]
            for t in range(1, SUB):
                solved = jnp.where(sub == t, rows[t], solved)
                diag = jnp.where(sub == t, entry[t][t], diag)
            slabs[now] = solved
            pivots[p][now] = diag
            weights = [rows[s] * inverse[s] for s in range(SUB)]
            for s in range(SUB - 1, -1, -1):
                for t in range(s + 1, SUB):
                    weights[s] = weights[s] - factor[t, s] * weights[t]
            for later in range(now + 1, count):
                terms = [spread(slabs[later], start, base + s) * weights[s] for s in range(SUB)]
                while len(terms) > 1:
                    terms = [a + b for a, b in zip(terms[::2], terms[1::2])]
                slabs[later] = jnp.where(inside, 0.0, slabs[later]) - terms[0]
    for p, slabs in enumerate(pairs):
        for now in range(count):
            unit = jnp.where(inner < sub + now * SUB, slabs[now], jnp.where(inner == sub + now * SUB, 1.0, 0.0))
            slabs[now] = unit * lax.rsqrt(pivots[p][now])


def inverse_factor(work_ref, tile_ref, frags):
    size = work_ref.shape[1]
    for block in range(size // BLOCK):
        lo, hi = block * BLOCK, (block + 1) * BLOCK
        for i, f in enumerate(frags):
            left = (i % 2) * BLOCK
            tile_ref[i // 2, :, left : left + BLOCK] = work_ref[f, lo:hi, lo:hi]
        pairs = [[tile_ref[p, r : r + SUB, :] for r in range(0, BLOCK, SUB)] for p in range((len(frags) + 1) // 2)]
        invert_tiles(pairs)
        for p, slabs in enumerate(pairs):
            for r, slab in enumerate(slabs):
                tile_ref[p, r * SUB : (r + 1) * SUB, :] = slab
        yield block
        for i, f in enumerate(frags):
            left = (i % 2) * BLOCK
            inverse = tile_ref[i // 2, :, left : left + BLOCK]
            rows = jnp.dot(inverse, work_ref[f, lo:hi, :], precision=HIGH, preferred_element_type=jnp.float32)
            work_ref[f, lo:hi, :] = rows
            work_ref[f, lo:hi, lo:hi] = inverse
            if hi < size:
                below = jnp.transpose(rows)[hi:, :]
                work_ref[f, hi:, lo:hi] = jnp.zeros((size - hi, BLOCK), jnp.float32)
                work_ref[f, hi:, :] -= jnp.dot(
                    below, work_ref[f, lo:hi, :], precision=HIGH, preferred_element_type=jnp.float32
                )
        yield block


def kernel(
    nfrag_ref, nbath_ref, bath_ref, density_ref, index_ref, factor_ref, out_ref,
    initial, held, partial, gram, gram_in, tiles, outgoing, incoming, density, picked, summed, far, shares, index,
    send_sem, recv_sem, load_sem, gram_sem, value_sem, rows_sem, density_sem, share_sem,
):
    frags, depth, nbmax = bath_ref.shape
    local_rows = density.shape[0]
    nfmax = picked.shape[3]
    size = nfmax + nbmax
    piece = depth // 2
    aux, orb = lax.axis_index("aux"), lax.axis_index("orb")
    up, across = aux // SIDE, aux % SIDE

    def device(coord_up, coord_across):
        return {"aux": coord_up * SIDE + coord_across}

    def turn(value, by):
        return lax.rem(value + by + SIDE, SIDE)

    place = [(across, up), (up, across)]

    def neighbour(half, second, by):
        first, other = place[half]
        if second:
            other = turn(other, by)
        else:
            first = turn(first, by)
        return device(other, first) if half == 0 else device(first, other)

    frag = lax.axis_index("frag")
    high, core = frag // 2, frag % 2
    sibling = {"frag": high * 2 + 1 - core}
    opposite = {"frag": (1 - high) * 2 + core}
    ranks = SIDE * SIDE

    def rank(by):
        return lax.rem(aux + by + ranks, ranks)

    barrier = pltpu.get_barrier_semaphore()
    greeted = [{"aux": rank(by)} for by in range(1, ranks)] + [{"orb": 1 - orb}, sibling, opposite]
    for other in greeted:
        pl.semaphore_signal(barrier, inc=1, device_id=other, device_id_type=MESH)
    partner = {"orb": 1 - orb}
    fetch = pltpu.make_async_copy(density_ref, density, density_sem)
    fetch.start()

    units = [("bath", 0), ("bath", 1), ("rows", 0), ("rows", 1), ("bath", 2), ("rows", 2), ("bath", 3), ("rows", 3)]

    def span(unit):
        kind, f = units[unit]
        return f, (0 if kind == "rows" else nfmax), (nfmax if kind == "rows" else nbmax)

    def put(half, f, low, value):
        first, other = place[half]
        column = pl.multiple_of((other * SIDE + first) * piece, piece)
        initial[half, f, low : low + value.shape[0], pl.ds(column, piece)] = value

    def put_bath(f):
        for half in range(2):
            put(half, f, nfmax, jnp.transpose(bath_ref[f, half * piece : (half + 1) * piece, :]))

    column_index = jnp.transpose(index_ref[...].astype(jnp.float32))
    for f in range(frags):
        for place_of, group in enumerate((0, 2, 1, 3)):
            low = place_of * nfmax
            value = column_index[:, group * frags + f : group * frags + f + 1]
            index[f, low : low + nfmax, :] = jnp.broadcast_to(value, (nfmax, LANES)).astype(jnp.int32)
    for f in range(frags):
        put_bath(f)

    loads = []
    for half in range(2):
        for slot in range(SIDE * SIDE):
            other, first = slot // SIDE, slot % SIDE
            source = slot if half == 0 else first * SIDE + other
            loads.append(
                pltpu.make_async_copy(
                    factor_ref.at[source, half], held.at[half, slot], load_sem.at[half, slot]
                )
            )
            loads[-1].start()

    def region(unit, half, second, offset, part):
        f, low, count = span(unit)
        first, other = place[half]
        if part is not None:
            count = count // 2
            low = low + part * count
        if second:
            column, width = turn(other, offset) * SIDE * piece, SIDE * piece
        else:
            column, width = (other * SIDE + turn(first, offset)) * piece, piece
        column = pl.multiple_of(column, piece)
        return initial.at[half, f, low : low + count, pl.ds(column, width)]

    messages = [(0, None, 1), (0, None, -1), (-1, 0, 1), (1, 1, -1)]
    sent = []

    def message(unit, half, second, index):
        offset, part, by = messages[index]
        where = region(unit, half, second, offset, part)
        slot = (4 if second else 0) + index
        return pltpu.make_async_remote_copy(
            src_ref=where,
            dst_ref=where,
            send_sem=send_sem.at[unit, half, slot],
            recv_sem=recv_sem.at[unit, half, slot],
            device_id=neighbour(half, second, by),
            device_id_type=MESH,
        )

    def send(unit, half, second, index):
        copy = message(unit, half, second, index)
        copy.start()
        sent.append(copy)

    def receive(unit, half, second, index):
        offset, part, by = messages[index]
        where = region(unit, half, second, offset - by, part)
        slot = (4 if second else 0) + index
        pltpu.make_async_remote_copy(
            src_ref=where,
            dst_ref=where,
            send_sem=send_sem.at[unit, half, slot],
            recv_sem=recv_sem.at[unit, half, slot],
            device_id=neighbour(half, second, by),
            device_id_type=MESH,
        ).wait_recv()

    passed = set()

    def stage(number, unit):
        if unit >= len(units) or (number, unit) in passed:
            return
        passed.add((number, unit))
        second = number > 2
        for half in range(2):
            if number == 1:
                send(unit, half, False, 0)
                send(unit, half, False, 1)
            elif number in (2, 4):
                receive(unit, half, second, 0)
                send(unit, half, second, 2)
                receive(unit, half, second, 1)
                send(unit, half, second, 3)
            elif number == 3:
                receive(unit, half, False, 2)
                receive(unit, half, False, 3)
                send(unit, half, True, 0)
                send(unit, half, True, 1)
            else:
                receive(unit, half, True, 2)
                receive(unit, half, True, 3)

    def pick(f):
        step = 8 * LANES
        lane = lax.broadcasted_iota(jnp.int32, (index.shape[1], LANES), 1) + frag * local_rows

        def one(block, total):
            start = pl.multiple_of(block * step, step)
            hot = [
                jnp.where(index[f] == lane + (start + part * LANES), 1.0, 0.0).astype(jnp.bfloat16)
                for part in range(8)
            ]
            rows = density[pl.ds(start, step), :]
            return total + jnp.dot(jnp.concatenate(hot, axis=1), rows, preferred_element_type=jnp.float32)

        total = jnp.zeros((index.shape[1], depth), jnp.float32)
        total = lax.fori_loop(0, local_rows // step, one, total)
        picked[f] = total.astype(picked.dtype).reshape(picked.shape[1:])

    def sibling_copy(f):
        return pltpu.make_async_remote_copy(
            src_ref=picked.at[f, 1 - core],
            dst_ref=summed.at[f],
            send_sem=rows_sem.at[0, f],
            recv_sem=rows_sem.at[1, f],
            device_id=sibling,
            device_id_type=MESH,
        )

    def far_copy(f):
        return pltpu.make_async_remote_copy(
            src_ref=summed.at[f, 1 - high],
            dst_ref=far.at[f],
            send_sem=rows_sem.at[2, f],
            recv_sem=rows_sem.at[3, f],
            device_id=opposite,
            device_id_type=MESH,
        )

    def send_picked(f):
        sibling_copy(f).start()

    def add_sibling(f):
        sibling_copy(f).wait()
        summed[f] = summed[f] + picked[f, core]

    def send_far(f):
        far_copy(f).start()

    def take_rows(f):
        far_copy(f).wait()
        value = summed[f, high] + far[f]
        for half in range(2):
            put(half, f, 0, value[:, half * piece : (half + 1) * piece])

    contract = (((1,), (1,)), ((), ()))

    def make_gram(f):
        total = lax.dot_general(initial[0, f], initial[0, f], contract, preferred_element_type=jnp.float32)
        total += lax.dot_general(initial[1, f], initial[1, f], contract, preferred_element_type=jnp.float32)
        gram[f] = total

    def gram_copy(f):
        return pltpu.make_async_remote_copy(
            src_ref=gram.at[f],
            dst_ref=gram_in.at[f],
            send_sem=gram_sem.at[0, f],
            recv_sem=gram_sem.at[1, f],
            device_id=partner,
            device_id_type=MESH,
        )

    share = size // ranks
    early = frags - 1

    def my_share():
        return pl.ds(pl.multiple_of(aux * share, share), share)

    def early_gram():
        total = jnp.zeros((size, size), jnp.float32)
        for half in range(2):
            first, other = place[half]
            column = pl.multiple_of((other * SIDE + first) * piece, piece)
            block = initial[half, early, :, pl.ds(column, piece)]
            total += lax.dot_general(block, block, contract, preferred_element_type=jnp.float32)
        gram[early] = total

    def share_copy(by):
        rows_of = pl.ds(pl.multiple_of(rank(by) * share, share), share)
        return pltpu.make_async_remote_copy(
            src_ref=gram.at[early, rows_of, :],
            dst_ref=shares.at[by],
            send_sem=share_sem.at[0, by],
            recv_sem=share_sem.at[1, by],
            device_id={"aux": rank(by)},
            device_id_type=MESH,
        )

    def share_swap():
        return pltpu.make_async_remote_copy(
            src_ref=shares.at[0],
            dst_ref=shares.at[ranks],
            send_sem=share_sem.at[0, 0],
            recv_sem=share_sem.at[1, 0],
            device_id=partner,
            device_id_type=MESH,
        )

    def total_copy(by, source):
        rows_of = pl.ds(pl.multiple_of(rank(source) * share, share), share)
        return pltpu.make_async_remote_copy(
            src_ref=gram_in.at[early, rows_of, :],
            dst_ref=gram_in.at[early, rows_of, :],
            send_sem=share_sem.at[2, by],
            recv_sem=share_sem.at[3, by],
            device_id={"aux": rank(by)},
            device_id_type=MESH,
        )

    def early_send():
        for by in range(1, ranks):
            share_copy(by).start()

    def early_sum():
        for by in range(1, ranks):
            share_copy(by).wait()
        total = gram[early, my_share(), :]
        for by in range(1, ranks):
            total = total + shares[by]
        shares[0] = total

    def early_swap():
        share_swap().start()

    def early_total():
        share_swap().wait()
        gram_in[early, my_share(), :] = shares[0] + shares[ranks]

    def early_spread():
        for by in range(1, ranks):
            total_copy(by, 0).start()

    def early_take():
        for by in range(1, ranks):
            total_copy(by, 0).wait_send()
            total_copy(by, -by).wait_recv()

    width = 512
    tiles_q = partial.shape[2] // width

    def project(f, low=0, high_row=size, offsets=None):
        count = high_row - low

        def one(q, carry):
            column = pl.ds(pl.multiple_of(q * width, width), width)
            total = jnp.zeros((count, width), jnp.float32)
            if offsets is None:
                def add(half, total):
                    block = held[half, :, :, column].reshape(SIDE * SIDE * piece, width)
                    return total + jnp.dot(
                        initial[half, f, low:high_row], block, preferred_element_type=jnp.float32
                    )

                total = lax.fori_loop(0, 2, add, total)
            for half in range(0 if offsets is None else 2):
                for offset in offsets:
                    start = turn(place[half][1], offset) * SIDE
                    block = held[half, pl.ds(start, SIDE), :, column].reshape(SIDE * piece, width)
                    columns = pl.ds(pl.multiple_of(start * piece, piece), SIDE * piece)
                    total += jnp.dot(initial[half, f, low:high_row, columns], block, preferred_element_type=jnp.float32)
            if offsets is not None and offsets[0] != 0:
                total += partial[f, low:high_row, column]
            partial[f, low:high_row, column] = total
            return carry

        lax.fori_loop(0, tiles_q, one, 0)

    row = lax.broadcasted_iota(jnp.int32, (size, size), 0)
    col = lax.broadcasted_iota(jnp.int32, (size, size), 1)

    def both_live(f):
        fragment = frag * frags + f
        used, used_bath = nfrag_ref[fragment], nbath_ref[fragment] + nfmax
        live_row = (row < used) | ((row >= nfmax) & (row < used_bath))
        live_col = (col < used) | ((col >= nfmax) & (col < used_bath))
        return live_row & live_col

    def prepare(f):
        total = gram_in[f]
        if f != early:
            gram_copy(f).wait()
            total = gram[f] + gram_in[f]
        gram_in[f] = jnp.where(both_live(f), total, jnp.where(row == col, 1.0, 0.0))

    def value_copy(f):
        return pltpu.make_async_remote_copy(
            src_ref=outgoing.at[f],
            dst_ref=incoming.at[f],
            send_sem=value_sem.at[0, f],
            recv_sem=value_sem.at[1, f],
            device_id=partner,
            device_id_type=MESH,
        )

    def mask(f):
        gram_in[f] = jnp.where(both_live(f) & (row >= col), gram_in[f], 0.0)

    def apply(f):
        theirs = gram_in[f, pl.ds(pl.multiple_of((1 - orb) * nfmax, nfmax), nfmax), :]
        mine = gram_in[f, pl.ds(pl.multiple_of(orb * nfmax, nfmax), nfmax), :]
        value = jnp.dot(theirs, partial[f], precision=HIGH, preferred_element_type=jnp.float32)
        outgoing[f] = value.astype(outgoing.dtype)
        value = jnp.dot(mine, partial[f], precision=HIGH, preferred_element_type=jnp.float32)
        value_copy(f).start()
        partial[f, :nfmax, :] = value

    def finish(f):
        value_copy(f).wait()
        out_ref[f] = (partial[f, :nfmax, :] + incoming[f].astype(jnp.float32)).astype(out_ref.dtype)

    pl.semaphore_wait(barrier, len(greeted))
    stage(1, 0)
    stage(1, 1)
    stage(1, 4)
    fetch.wait()
    pick(0)
    stage(2, 0)
    stage(2, 1)
    stage(1, 6)
    send_picked(0)
    pick(2)
    stage(3, 0)
    pick(3)
    pick(1)
    add_sibling(0)
    send_picked(1)
    send_far(0)
    stage(3, 1)
    stage(4, 0)
    take_rows(0)
    send_picked(2)
    add_sibling(1)
    stage(1, 2)
    send_far(1)
    send_picked(3)
    stage(4, 1)
    stage(2, 2)
    take_rows(1)
    for copy in loads:
        copy.wait()
    stage(5, 0)
    stage(1, 3)
    stage(3, 2)
    add_sibling(2)
    stage(5, 1)
    send_far(2)
    add_sibling(3)
    stage(2, 4)
    stage(2, 3)
    send_far(3)
    take_rows(2)
    stage(4, 2)
    stage(3, 3)
    take_rows(3)
    stage(5, 2)
    make_gram(0)
    early_gram()
    project(0, 0, nfmax)
    stage(1, 5)
    stage(4, 3)
    gram_copy(0).start()
    project(1, nfmax, size)
    early_send()
    stage(5, 3)
    stage(2, 5)
    make_gram(1)
    stage(3, 4)
    stage(1, 7)
    gram_copy(1).start()
    stage(3, 5)
    prepare(0)
    project(1, 0, nfmax)
    early_sum()
    prepare(1)
    steps = inverse_factor(gram_in, tiles, [0,1])
    next(steps)
    next(steps)
    next(steps)
    stage(4, 4)
    next(steps)
    early_swap()
    next(steps)
    next(steps)
    stage(4, 5)
    next(steps)
    early_total()
    next(steps)
    stage(2, 6)
    mask(1)
    stage(5, 4)
    project(2, nfmax, size)
    stage(2, 7)
    early_spread()
    stage(5, 5)
    make_gram(2)
    mask(0)
    gram_copy(2).start()
    stage(3, 6)
    apply(1)
    project(0, nfmax, size)
    early_take()
    apply(0)
    prepare(3)
    project(2, 0, nfmax)
    stage(3, 7)
    prepare(2)
    steps = inverse_factor(gram_in, tiles, [2,3])
    next(steps)
    next(steps)
    next(steps)
    next(steps)
    stage(4, 6)
    next(steps)
    next(steps)
    next(steps)
    stage(4, 7)
    next(steps)
    mask(2)
    apply(2)
    project(3, 0, nfmax, (0,))
    project(3, 0, nfmax, (-1,1))
    stage(5, 6)
    stage(5, 7)
    mask(3)
    project(3, nfmax, size)
    project(3, 0, nfmax, (2,))
    apply(3)
    finish(0)
    finish(2)
    finish(1)
    finish(3)
    for copy in sent:
        copy.wait_send()


def fused(nfrag, nbath, bath, density, index, factor):
    frags, depth, nbmax = bath.shape
    local_rows = density.shape[0]
    total_frags, nfmax = index.shape
    groups = total_frags // frags
    size = nfmax + nbmax
    columns = factor.shape[1]
    ranks, piece = SIDE * SIDE, depth // 2
    sems = pltpu.SemaphoreType.DMA
    half_rows = size // 2
    vmem = pltpu.VMEM
    return pl.pallas_call(
        kernel,
        out_shape=jax.ShapeDtypeStruct((frags, half_rows, columns), jnp.bfloat16),
        in_specs=[
            pl.BlockSpec(memory_space=kind)
            for kind in (pltpu.SMEM, pltpu.SMEM, vmem, pl.ANY, vmem, pl.ANY)
        ],
        out_specs=pl.BlockSpec(memory_space=vmem),
        scratch_shapes=[
            vmem((2, frags, size, ranks * piece), jnp.bfloat16),
            vmem((2, ranks, piece, columns), jnp.bfloat16),
            vmem((frags, size, columns), jnp.float32),
            vmem((frags, size, size), jnp.float32),
            vmem((frags, size, size), jnp.float32),
            vmem((2, BLOCK, LANES), jnp.float32),
            vmem((frags, half_rows, columns), jnp.bfloat16),
            vmem((frags, half_rows, columns), jnp.bfloat16),
            vmem((local_rows, depth), jnp.bfloat16),
            vmem((frags, 2, groups // 2, nfmax, depth), jnp.bfloat16),
            vmem((frags, groups // 2, nfmax, depth), jnp.bfloat16),
            vmem((frags, nfmax, depth), jnp.bfloat16),
            vmem((ranks + 1, size // ranks, size), jnp.float32),
            vmem((frags, groups * nfmax, LANES), jnp.int32),
            sems((2 * frags, 2, 8)),
            sems((2 * frags, 2, 8)),
            sems((2, ranks)),
            sems((2, frags)),
            sems((2, frags)),
            sems((4, frags)),
            sems(()),
            sems((4, ranks)),
        ],
        compiler_params=pltpu.CompilerParams(
            collective_id=0, has_side_effects=True, vmem_limit_bytes=63 * 1024 * 1024
        ),
    )(nfrag, nbath, bath, density, index, factor.reshape(ranks, 2, piece, columns))


def per_device(density, bath, factor, frag_index, nfrag, nbath):
    local_rows, _, depth = density.shape
    frags, _, _, nbmax = bath.shape
    return fused(
        nfrag, nbath, bath.reshape(frags, depth, nbmax), density.reshape(local_rows, depth), frag_index, factor
    )


def solution(mesh):
    placed = (
        P("frag", "orb", "aux"),
        P("frag", "orb", "aux", None),
        P("orb", "aux"),
        P(),
        P(),
        P(),
    )
    return jax.shard_map(
        per_device, mesh=mesh, in_specs=placed, out_specs=P("frag", "orb", "aux"), check_vma=False
    )
```

```python
import functools

import jax
import jax.numpy as jnp
from jax import lax
from jax.experimental import pallas as pl
from jax.experimental.pallas import tpu as pltpu
from jax.sharding import PartitionSpec as P

HIGH = lax.Precision.HIGHEST
MESH = pl.DeviceIdType.MESH
BLOCK = 64
SUB = 8
LANES = 128
SIDE = 4

def spread(value, start, j):
    return jnp.take_along_axis(value, start + j, axis=1)

def invert_tiles(pairs):
    lane = lax.broadcasted_iota(jnp.int32, (SUB, LANES), 1)
    sub = lax.broadcasted_iota(jnp.int32, (SUB, LANES), 0)
    inner = lane % BLOCK
    start = lane - inner
    count = BLOCK // SUB
    pivots = [[None] * count for _ in pairs]
    for now in range(count):
        base = now * SUB
        inside = (inner >= base) & (inner < base + SUB)
        for p, slabs in enumerate(pairs):
            rows = [jnp.broadcast_to(slabs[now][t : t + 1], (SUB, LANES)) for t in range(SUB)]
            entry = [[spread(rows[t], start, base + s) for s in range(t + 1)] for t in range(SUB)]
            rows = [jnp.where(inside, jnp.where(inner == base + t, 1.0, 0.0), rows[t]) for t in range(SUB)]
            inverse, factor = [], {}
            for s in range(SUB):
                inverse.append(1.0 / entry[s][s])
                for t in range(s + 1, SUB):
                    factor[t, s] = entry[t][s] * inverse[s]
                for t in range(s + 1, SUB):
                    for u in range(s + 1, t + 1):
                        entry[t][u] = entry[t][u] - factor[t, s] * entry[u][s]
                for t in range(s + 1, SUB):
                    rows[t] = rows[t] - factor[t, s] * rows[s]
            solved, diag = rows[0], entry[0][0]
            for t in range(1, SUB):
                solved = jnp.where(sub == t, rows[t], solved)
                diag = jnp.where(sub == t, entry[t][t], diag)
            slabs[now] = solved
            pivots[p][now] = diag
            weights = [rows[s] * inverse[s] for s in range(SUB)]
            for s in range(SUB - 1, -1, -1):
                for t in range(s + 1, SUB):
                    weights[s] = weights[s] - factor[t, s] * weights[t]
            for later in range(now + 1, count):
                terms = [spread(slabs[later], start, base + s) * weights[s] for s in range(SUB)]
                while len(terms) > 1:
                    terms = [a + b for a, b in zip(terms[::2], terms[1::2])]
                slabs[later] = jnp.where(inside, 0.0, slabs[later]) - terms[0]
    for p, slabs in enumerate(pairs):
        for now in range(count):
            unit = jnp.where(inner < sub + now * SUB, slabs[now], jnp.where(inner == sub + now * SUB, 1.0, 0.0))
            slabs[now] = unit * lax.rsqrt(pivots[p][now])


def inverse_factor(work_ref, tile_ref, frags):
    size = work_ref.shape[1]
    for block in range(size // BLOCK):
        lo, hi = block * BLOCK, (block + 1) * BLOCK
        for i, f in enumerate(frags):
            left = (i % 2) * BLOCK
            tile_ref[i // 2, :, left : left + BLOCK] = work_ref[f, lo:hi, lo:hi]
        pairs = [[tile_ref[p, r : r + SUB, :] for r in range(0, BLOCK, SUB)] for p in range((len(frags) + 1) // 2)]
        invert_tiles(pairs)
        for p, slabs in enumerate(pairs):
            for r, slab in enumerate(slabs):
                tile_ref[p, r * SUB : (r + 1) * SUB, :] = slab
        yield block
        for i, f in enumerate(frags):
            left = (i % 2) * BLOCK
            inverse = tile_ref[i // 2, :, left : left + BLOCK]
            rows = jnp.dot(inverse, work_ref[f, lo:hi, :], precision=HIGH, preferred_element_type=jnp.float32)
            work_ref[f, lo:hi, :] = rows
            work_ref[f, lo:hi, lo:hi] = inverse
            if hi < size:
                below = jnp.transpose(rows)[hi:, :]
                work_ref[f, hi:, lo:hi] = jnp.zeros((size - hi, BLOCK), jnp.float32)
                work_ref[f, hi:, :] -= jnp.dot(
                    below, work_ref[f, lo:hi, :], precision=HIGH, preferred_element_type=jnp.float32
                )
        yield block


def kernel(
    nfrag_ref, nbath_ref, bath_ref, density_ref, index_ref, factor_ref, out_ref,
    initial, held, partial, gram, gram_in, tiles, outgoing, incoming, density, picked, summed, far, shares, index,
    send_sem, recv_sem, load_sem, gram_sem, value_sem, rows_sem, density_sem, share_sem,
):
    frags, depth, nbmax = bath_ref.shape
    local_rows = density.shape[0]
    nfmax = picked.shape[3]
    size = nfmax + nbmax
    piece = depth // 2
    aux, orb = lax.axis_index("aux"), lax.axis_index("orb")
    up, across = aux // SIDE, aux % SIDE

    def device(coord_up, coord_across):
        return {"aux": coord_up * SIDE + coord_across}

    def turn(value, by):
        return lax.rem(value + by + SIDE, SIDE)

    place = [(across, up), (up, across)]

    def neighbour(half, second, by):
        first, other = place[half]
        if second:
            other = turn(other, by)
        else:
            first = turn(first, by)
        return device(other, first) if half == 0 else device(first, other)

    frag = lax.axis_index("frag")
    high, core = frag // 2, frag % 2
    sibling = {"frag": high * 2 + 1 - core}
    opposite = {"frag": (1 - high) * 2 + core}
    ranks = SIDE * SIDE

    def rank(by):
        return lax.rem(aux + by + ranks, ranks)

    barrier = pltpu.get_barrier_semaphore()
    greeted = [{"aux": rank(by)} for by in range(1, ranks)] + [{"orb": 1 - orb}, sibling, opposite]
    for other in greeted:
        pl.semaphore_signal(barrier, inc=1, device_id=other, device_id_type=MESH)
    partner = {"orb": 1 - orb}
    fetch = pltpu.make_async_copy(density_ref, density, density_sem)
    fetch.start()

    units = [("bath", 0), ("bath", 1), ("rows", 0), ("rows", 1), ("bath", 2), ("rows", 2), ("bath", 3), ("rows", 3)]

    def span(unit):
        kind, f = units[unit]
        return f, (0 if kind == "rows" else nfmax), (nfmax if kind == "rows" else nbmax)

    def put(half, f, low, value):
        first, other = place[half]
        column = pl.multiple_of((other * SIDE + first) * piece, piece)
        initial[half, f, low : low + value.shape[0], pl.ds(column, piece)] = value

    def put_bath(f):
        for half in range(2):
            put(half, f, nfmax, jnp.transpose(bath_ref[f, half * piece : (half + 1) * piece, :]))

    def put_index():
        column_index = jnp.transpose(index_ref[...].astype(jnp.float32))
        for f in range(frags):
            for place_of, group in enumerate((0, 2, 1, 3)):
                low = place_of * nfmax
                value = column_index[:, group * frags + f : group * frags + f + 1]
                index[f, low : low + nfmax, :] = jnp.broadcast_to(value, (nfmax, LANES)).astype(jnp.int32)

    for f in range(2):
        put_bath(f)

    loads = []
    for half in range(2):
        for slot in range(SIDE * SIDE):
            other, first = slot // SIDE, slot % SIDE
            source = slot if half == 0 else first * SIDE + other
            loads.append(
                pltpu.make_async_copy(
                    factor_ref.at[source, half], held.at[half, slot], load_sem.at[half, slot]
                )
            )
            loads[-1].start()

    def region(unit, half, second, offset, part):
        f, low, count = span(unit)
        first, other = place[half]
        if part is not None:
            count = count // 2
            low = low + part * count
        if second:
            column, width = turn(other, offset) * SIDE * piece, SIDE * piece
        else:
            column, width = (other * SIDE + turn(first, offset)) * piece, piece
        column = pl.multiple_of(column, piece)
        return initial.at[half, f, low : low + count, pl.ds(column, width)]

    messages = [(0, None, 1), (0, None, -1), (-1, 0, 1), (1, 1, -1)]
    sent = []

    def message(unit, half, second, index):
        offset, part, by = messages[index]
        where = region(unit, half, second, offset, part)
        slot = (4 if second else 0) + index
        return pltpu.make_async_remote_copy(
            src_ref=where,
            dst_ref=where,
            send_sem=send_sem.at[unit, half, slot],
            recv_sem=recv_sem.at[unit, half, slot],
            device_id=neighbour(half, second, by),
            device_id_type=MESH,
        )

    def send(unit, half, second, index):
        copy = message(unit, half, second, index)
        copy.start()
        sent.append(copy)

    def receive(unit, half, second, index):
        offset, part, by = messages[index]
        where = region(unit, half, second, offset - by, part)
        slot = (4 if second else 0) + index
        pltpu.make_async_remote_copy(
            src_ref=where,
            dst_ref=where,
            send_sem=send_sem.at[unit, half, slot],
            recv_sem=recv_sem.at[unit, half, slot],
            device_id=neighbour(half, second, by),
            device_id_type=MESH,
        ).wait_recv()

    passed = set()

    def stage(number, unit):
        if unit >= len(units) or (number, unit) in passed:
            return
        passed.add((number, unit))
        second = number > 2
        for half in range(2):
            if number == 1:
                send(unit, half, False, 0)
                send(unit, half, False, 1)
            elif number in (2, 4):
                receive(unit, half, second, 0)
                send(unit, half, second, 2)
                receive(unit, half, second, 1)
                send(unit, half, second, 3)
            elif number == 3:
                receive(unit, half, False, 2)
                receive(unit, half, False, 3)
                send(unit, half, True, 0)
                send(unit, half, True, 1)
            else:
                receive(unit, half, True, 2)
                receive(unit, half, True, 3)

    def pick(f):
        step = 8 * LANES
        lane = lax.broadcasted_iota(jnp.int32, (index.shape[1], LANES), 1) + frag * local_rows

        def one(block, total):
            start = pl.multiple_of(block * step, step)
            hot = [
                jnp.where(index[f] == lane + (start + part * LANES), 1.0, 0.0).astype(jnp.bfloat16)
                for part in range(8)
            ]
            rows = density[pl.ds(start, step), :]
            return total + jnp.dot(jnp.concatenate(hot, axis=1), rows, preferred_element_type=jnp.float32)

        total = jnp.zeros((index.shape[1], depth), jnp.float32)
        total = lax.fori_loop(0, local_rows // step, one, total)
        picked[f] = total.astype(picked.dtype).reshape(picked.shape[1:])

    def sibling_copy(f):
        return pltpu.make_async_remote_copy(
            src_ref=picked.at[f, 1 - core],
            dst_ref=summed.at[f],
            send_sem=rows_sem.at[0, f],
            recv_sem=rows_sem.at[1, f],
            device_id=sibling,
            device_id_type=MESH,
        )

    def far_copy(f):
        return pltpu.make_async_remote_copy(
            src_ref=summed.at[f, 1 - high],
            dst_ref=far.at[f],
            send_sem=rows_sem.at[2, f],
            recv_sem=rows_sem.at[3, f],
            device_id=opposite,
            device_id_type=MESH,
        )

    def send_picked(f):
        sibling_copy(f).start()

    def add_sibling(f):
        sibling_copy(f).wait()
        summed[f] = summed[f] + picked[f, core]

    def send_far(f):
        far_copy(f).start()

    def take_rows(f):
        far_copy(f).wait()
        value = summed[f, high] + far[f]
        for half in range(2):
            put(half, f, 0, value[:, half * piece : (half + 1) * piece])

    contract = (((1,), (1,)), ((), ()))

    def make_gram(f):
        total = lax.dot_general(initial[0, f], initial[0, f], contract, preferred_element_type=jnp.float32)
        total += lax.dot_general(initial[1, f], initial[1, f], contract, preferred_element_type=jnp.float32)
        gram[f] = total

    def gram_copy(f):
        return pltpu.make_async_remote_copy(
            src_ref=gram.at[f],
            dst_ref=gram_in.at[f],
            send_sem=gram_sem.at[0, f],
            recv_sem=gram_sem.at[1, f],
            device_id=partner,
            device_id_type=MESH,
        )

    share = size // ranks
    early = frags - 1

    def my_share():
        return pl.ds(pl.multiple_of(aux * share, share), share)

    def early_gram():
        total = jnp.zeros((size, size), jnp.float32)
        for half in range(2):
            first, other = place[half]
            column = pl.multiple_of((other * SIDE + first) * piece, piece)
            block = initial[half, early, :, pl.ds(column, piece)]
            total += lax.dot_general(block, block, contract, preferred_element_type=jnp.float32)
        gram[early] = total

    def share_copy(by):
        rows_of = pl.ds(pl.multiple_of(rank(by) * share, share), share)
        return pltpu.make_async_remote_copy(
            src_ref=gram.at[early, rows_of, :],
            dst_ref=shares.at[by],
            send_sem=share_sem.at[0, by],
            recv_sem=share_sem.at[1, by],
            device_id={"aux": rank(by)},
            device_id_type=MESH,
        )

    def share_swap():
        return pltpu.make_async_remote_copy(
            src_ref=shares.at[0],
            dst_ref=shares.at[ranks],
            send_sem=share_sem.at[0, 0],
            recv_sem=share_sem.at[1, 0],
            device_id=partner,
            device_id_type=MESH,
        )

    def total_copy(by, source):
        rows_of = pl.ds(pl.multiple_of(rank(source) * share, share), share)
        return pltpu.make_async_remote_copy(
            src_ref=gram_in.at[early, rows_of, :],
            dst_ref=gram_in.at[early, rows_of, :],
            send_sem=share_sem.at[2, by],
            recv_sem=share_sem.at[3, by],
            device_id={"aux": rank(by)},
            device_id_type=MESH,
        )

    def early_send():
        for by in range(1, ranks):
            share_copy(by).start()

    def early_sum():
        for by in range(1, ranks):
            share_copy(by).wait()
        total = gram[early, my_share(), :]
        for by in range(1, ranks):
            total = total + shares[by]
        shares[0] = total

    def early_swap():
        share_swap().start()

    def early_total():
        share_swap().wait()
        gram_in[early, my_share(), :] = shares[0] + shares[ranks]

    def early_spread():
        for by in range(1, ranks):
            total_copy(by, 0).start()

    def early_take():
        for by in range(1, ranks):
            total_copy(by, 0).wait_send()
            total_copy(by, -by).wait_recv()

    width = 512
    tiles_q = partial.shape[2] // width

    def project(f, low=0, high_row=size, offsets=None):
        count = high_row - low

        def one(q, carry):
            column = pl.ds(pl.multiple_of(q * width, width), width)
            total = jnp.zeros((count, width), jnp.float32)
            if offsets is None:
                def add(half, total):
                    block = held[half, :, :, column].reshape(SIDE * SIDE * piece, width)
                    return total + jnp.dot(
                        initial[half, f, low:high_row], block, preferred_element_type=jnp.float32
                    )

                total = lax.fori_loop(0, 2, add, total)
            for half in range(0 if offsets is None else 2):
                for offset in offsets:
                    start = turn(place[half][1], offset) * SIDE
                    block = held[half, pl.ds(start, SIDE), :, column].reshape(SIDE * piece, width)
                    columns = pl.ds(pl.multiple_of(start * piece, piece), SIDE * piece)
                    total += jnp.dot(initial[half, f, low:high_row, columns], block, preferred_element_type=jnp.float32)
            if offsets is not None and offsets[0] != 0:
                total += partial[f, low:high_row, column]
            partial[f, low:high_row, column] = total
            return carry

        lax.fori_loop(0, tiles_q, one, 0)

    row = lax.broadcasted_iota(jnp.int32, (size, size), 0)
    col = lax.broadcasted_iota(jnp.int32, (size, size), 1)

    def both_live(f):
        fragment = frag * frags + f
        used, used_bath = nfrag_ref[fragment], nbath_ref[fragment] + nfmax
        live_row = (row < used) | ((row >= nfmax) & (row < used_bath))
        live_col = (col < used) | ((col >= nfmax) & (col < used_bath))
        return live_row & live_col

    def prepare(f):
        total = gram_in[f]
        if f != early:
            gram_copy(f).wait()
            total = gram[f] + gram_in[f]
        gram_in[f] = jnp.where(both_live(f), total, jnp.where(row == col, 1.0, 0.0))

    def value_copy(f):
        return pltpu.make_async_remote_copy(
            src_ref=outgoing.at[f],
            dst_ref=incoming.at[f],
            send_sem=value_sem.at[0, f],
            recv_sem=value_sem.at[1, f],
            device_id=partner,
            device_id_type=MESH,
        )

    def mask(f):
        gram_in[f] = jnp.where(both_live(f) & (row >= col), gram_in[f], 0.0)

    def apply(f):
        theirs = gram_in[f, pl.ds(pl.multiple_of((1 - orb) * nfmax, nfmax), nfmax), :]
        mine = gram_in[f, pl.ds(pl.multiple_of(orb * nfmax, nfmax), nfmax), :]
        value = jnp.dot(theirs, partial[f], precision=HIGH, preferred_element_type=jnp.float32)
        outgoing[f] = value.astype(outgoing.dtype)
        value = jnp.dot(mine, partial[f], precision=HIGH, preferred_element_type=jnp.float32)
        value_copy(f).start()
        partial[f, :nfmax, :] = value

    def finish(f):
        value_copy(f).wait()
        out_ref[f] = (partial[f, :nfmax, :] + incoming[f].astype(jnp.float32)).astype(out_ref.dtype)

    pl.semaphore_wait(barrier, len(greeted))
    stage(1, 0)
    put_bath(2)
    fetch.wait()
    put_index()
    stage(1, 4)
    put_bath(3)
    stage(2, 0)
    stage(1, 1)
    pick(0)
    stage(3, 0)
    send_picked(0)
    pick(1)
    stage(2, 1)
    send_picked(1)
    stage(4, 0)
    add_sibling(0)
    stage(3, 1)
    send_far(0)
    stage(5, 0)
    pick(2)
    take_rows(0)
    add_sibling(1)
    send_picked(2)
    stage(1, 2)
    stage(4, 1)
    send_far(1)
    for copy in loads:
        copy.wait()
    pick(3)
    stage(2, 2)
    stage(2, 4)
    stage(3, 2)
    send_picked(3)
    take_rows(1)
    add_sibling(2)
    stage(1, 3)
    send_far(2)
    project(0, nfmax, size)
    stage(1, 6)
    stage(2, 3)
    stage(3, 3)
    stage(5, 1)
    add_sibling(3)
    take_rows(2)
    stage(4, 2)
    send_far(3)
    stage(4, 3)
    stage(1, 5)
    take_rows(3)
    stage(5, 2)
    make_gram(0)
    early_gram()
    gram_copy(0).start()
    stage(3, 4)
    early_send()
    stage(5, 3)
    project(0, 0, nfmax)
    make_gram(1)
    stage(2, 5)
    gram_copy(1).start()
    stage(1, 7)
    project(1, 0, nfmax)
    prepare(0)
    project(1, nfmax, size)
    early_sum()
    stage(3, 5)
    stage(4, 4)
    prepare(1)
    steps = inverse_factor(gram_in, tiles, [0,1])
    next(steps)
    next(steps)
    next(steps)
    next(steps)
    early_swap()
    next(steps)
    stage(4, 5)
    next(steps)
    stage(2, 7)
    next(steps)
    next(steps)
    stage(5, 4)
    early_total()
    stage(2, 6)
    stage(5, 5)
    early_spread()
    make_gram(2)
    stage(3, 7)
    gram_copy(2).start()
    project(2, nfmax, size)
    project(2, 0, nfmax)
    mask(0)
    early_take()
    project(3, 0, nfmax, (0,))
    mask(1)
    stage(3, 6)
    prepare(3)
    apply(0)
    prepare(2)
    steps = inverse_factor(gram_in, tiles, [2,3])
    next(steps)
    next(steps)
    apply(1)
    next(steps)
    next(steps)
    next(steps)
    stage(4, 6)
    next(steps)
    stage(4, 7)
    next(steps)
    next(steps)
    mask(2)
    apply(2)
    project(3, 0, nfmax, (-1,1))
    stage(5, 6)
    project(3, nfmax, size)
    stage(5, 7)
    project(3, 0, nfmax, (2,))
    mask(3)
    apply(3)
    finish(2)
    finish(0)
    finish(1)
    finish(3)
    for copy in sent:
        copy.wait_send()


def fused(nfrag, nbath, bath, density, index, factor):
    frags, depth, nbmax = bath.shape
    local_rows = density.shape[0]
    total_frags, nfmax = index.shape
    groups = total_frags // frags
    size = nfmax + nbmax
    columns = factor.shape[1]
    ranks, piece = SIDE * SIDE, depth // 2
    sems = pltpu.SemaphoreType.DMA
    half_rows = size // 2
    vmem = pltpu.VMEM
    return pl.pallas_call(
        kernel,
        out_shape=jax.ShapeDtypeStruct((frags, half_rows, columns), jnp.bfloat16),
        in_specs=[
            pl.BlockSpec(memory_space=kind)
            for kind in (pltpu.SMEM, pltpu.SMEM, vmem, pl.ANY, vmem, pl.ANY)
        ],
        out_specs=pl.BlockSpec(memory_space=vmem),
        scratch_shapes=[
            vmem((2, frags, size, ranks * piece), jnp.bfloat16),
            vmem((2, ranks, piece, columns), jnp.bfloat16),
            vmem((frags, size, columns), jnp.float32),
            vmem((frags, size, size), jnp.float32),
            vmem((frags, size, size), jnp.float32),
            vmem((2, BLOCK, LANES), jnp.float32),
            vmem((frags, half_rows, columns), jnp.bfloat16),
            vmem((frags, half_rows, columns), jnp.bfloat16),
            vmem((local_rows, depth), jnp.bfloat16),
            vmem((frags, 2, groups // 2, nfmax, depth), jnp.bfloat16),
            vmem((frags, groups // 2, nfmax, depth), jnp.bfloat16),
            vmem((frags, nfmax, depth), jnp.bfloat16),
            vmem((ranks + 1, size // ranks, size), jnp.float32),
            vmem((frags, groups * nfmax, LANES), jnp.int32),
            sems((2 * frags, 2, 8)),
            sems((2 * frags, 2, 8)),
            sems((2, ranks)),
            sems((2, frags)),
            sems((2, frags)),
            sems((4, frags)),
            sems(()),
            sems((4, ranks)),
        ],
        compiler_params=pltpu.CompilerParams(
            collective_id=0, has_side_effects=True, vmem_limit_bytes=63 * 1024 * 1024
        ),
    )(nfrag, nbath, bath, density, index, factor.reshape(ranks, 2, piece, columns))


def per_device(density, bath, factor, frag_index, nfrag, nbath):
    local_rows, _, depth = density.shape
    frags, _, _, nbmax = bath.shape
    return fused(
        nfrag, nbath, bath.reshape(frags, depth, nbmax), density.reshape(local_rows, depth), frag_index, factor
    )


def solution(mesh):
    placed = (
        P("frag", "orb", "aux"),
        P("frag", "orb", "aux", None),
        P("orb", "aux"),
        P(),
        P(),
        P(),
    )
    return jax.shard_map(
        per_device, mesh=mesh, in_specs=placed, out_specs=P("frag", "orb", "aux"), check_vma=False
    )
```

```python
import functools

import jax
import jax.numpy as jnp
from jax import lax
from jax.experimental import pallas as pl
from jax.experimental.pallas import tpu as pltpu
from jax.sharding import PartitionSpec as P

HIGH = lax.Precision.HIGHEST
MESH = pl.DeviceIdType.MESH
BLOCK = 64
SUB = 8
LANES = 128
SIDE = 4

def spread(value, start, j):
    return jnp.take_along_axis(value, start + j, axis=1)

def invert_tiles(pairs):
    lane = lax.broadcasted_iota(jnp.int32, (SUB, LANES), 1)
    sub = lax.broadcasted_iota(jnp.int32, (SUB, LANES), 0)
    inner = lane % BLOCK
    start = lane - inner
    count = BLOCK // SUB
    pivots = [[None] * count for _ in pairs]
    for now in range(count):
        base = now * SUB
        inside = (inner >= base) & (inner < base + SUB)
        for p, slabs in enumerate(pairs):
            rows = [jnp.broadcast_to(slabs[now][t : t + 1], (SUB, LANES)) for t in range(SUB)]
            entry = [[spread(rows[t], start, base + s) for s in range(t + 1)] for t in range(SUB)]
            rows = [jnp.where(inside, jnp.where(inner == base + t, 1.0, 0.0), rows[t]) for t in range(SUB)]
            inverse, factor = [], {}
            for s in range(SUB):
                inverse.append(1.0 / entry[s][s])
                for t in range(s + 1, SUB):
                    factor[t, s] = entry[t][s] * inverse[s]
                for t in range(s + 1, SUB):
                    for u in range(s + 1, t + 1):
                        entry[t][u] = entry[t][u] - factor[t, s] * entry[u][s]
                for t in range(s + 1, SUB):
                    rows[t] = rows[t] - factor[t, s] * rows[s]
            solved, diag = rows[0], entry[0][0]
            for t in range(1, SUB):
                solved = jnp.where(sub == t, rows[t], solved)
                diag = jnp.where(sub == t, entry[t][t], diag)
            slabs[now] = solved
            pivots[p][now] = diag
            weights = [rows[s] * inverse[s] for s in range(SUB)]
            for s in range(SUB - 1, -1, -1):
                for t in range(s + 1, SUB):
                    weights[s] = weights[s] - factor[t, s] * weights[t]
            for later in range(now + 1, count):
                terms = [spread(slabs[later], start, base + s) * weights[s] for s in range(SUB)]
                while len(terms) > 1:
                    terms = [a + b for a, b in zip(terms[::2], terms[1::2])]
                slabs[later] = jnp.where(inside, 0.0, slabs[later]) - terms[0]
    for p, slabs in enumerate(pairs):
        for now in range(count):
            unit = jnp.where(inner < sub + now * SUB, slabs[now], jnp.where(inner == sub + now * SUB, 1.0, 0.0))
            slabs[now] = unit * lax.rsqrt(pivots[p][now])


def inverse_factor(work_ref, tile_ref, frags):
    size = work_ref.shape[1]
    for block in range(size // BLOCK):
        lo, hi = block * BLOCK, (block + 1) * BLOCK
        for i, f in enumerate(frags):
            left = (i % 2) * BLOCK
            tile_ref[i // 2, :, left : left + BLOCK] = work_ref[f, lo:hi, lo:hi]
        pairs = [[tile_ref[p, r : r + SUB, :] for r in range(0, BLOCK, SUB)] for p in range((len(frags) + 1) // 2)]
        invert_tiles(pairs)
        for p, slabs in enumerate(pairs):
            for r, slab in enumerate(slabs):
                tile_ref[p, r * SUB : (r + 1) * SUB, :] = slab
        yield block
        for i, f in enumerate(frags):
            left = (i % 2) * BLOCK
            inverse = tile_ref[i // 2, :, left : left + BLOCK]
            rows = jnp.dot(inverse, work_ref[f, lo:hi, :], precision=HIGH, preferred_element_type=jnp.float32)
            work_ref[f, lo:hi, :] = rows
            work_ref[f, lo:hi, lo:hi] = inverse
            if hi < size:
                below = jnp.transpose(rows)[hi:, :]
                work_ref[f, hi:, lo:hi] = jnp.zeros((size - hi, BLOCK), jnp.float32)
                work_ref[f, hi:, :] -= jnp.dot(
                    below, work_ref[f, lo:hi, :], precision=HIGH, preferred_element_type=jnp.float32
                )
        yield block


def kernel(
    nfrag_ref, nbath_ref, bath_ref, density_ref, index_ref, factor_ref, out_ref,
    initial, held, partial, gram, gram_in, tiles, outgoing, incoming, density, picked, summed, far, shares, index,
    send_sem, recv_sem, load_sem, gram_sem, value_sem, rows_sem, density_sem, share_sem,
):
    frags, depth, nbmax = bath_ref.shape
    local_rows = density.shape[0]
    nfmax = picked.shape[3]
    size = nfmax + nbmax
    piece = depth // 2
    aux, orb = lax.axis_index("aux"), lax.axis_index("orb")
    up, across = aux // SIDE, aux % SIDE

    def device(coord_up, coord_across):
        return {"aux": coord_up * SIDE + coord_across}

    def turn(value, by):
        return lax.rem(value + by + SIDE, SIDE)

    place = [(across, up), (up, across)]

    def neighbour(half, second, by):
        first, other = place[half]
        if second:
            other = turn(other, by)
        else:
            first = turn(first, by)
        return device(other, first) if half == 0 else device(first, other)

    frag = lax.axis_index("frag")
    high, core = frag // 2, frag % 2
    sibling = {"frag": high * 2 + 1 - core}
    opposite = {"frag": (1 - high) * 2 + core}
    ranks = SIDE * SIDE

    def rank(by):
        return lax.rem(aux + by + ranks, ranks)

    barrier = pltpu.get_barrier_semaphore()
    greeted = [{"aux": rank(by)} for by in range(1, ranks)] + [{"orb": 1 - orb}, sibling, opposite]
    for other in greeted:
        pl.semaphore_signal(barrier, inc=1, device_id=other, device_id_type=MESH)
    partner = {"orb": 1 - orb}
    fetch = pltpu.make_async_copy(density_ref, density, density_sem)
    fetch.start()

    units = [("bath", 0), ("bath", 1), ("rows", 0), ("rows", 1), ("bath", 2), ("rows", 2), ("bath", 3), ("rows", 3)]

    def span(unit):
        kind, f = units[unit]
        return f, (0 if kind == "rows" else nfmax), (nfmax if kind == "rows" else nbmax)

    def put(half, f, low, value):
        first, other = place[half]
        column = pl.multiple_of((other * SIDE + first) * piece, piece)
        initial[half, f, low : low + value.shape[0], pl.ds(column, piece)] = value

    def put_bath(f):
        for half in range(2):
            put(half, f, nfmax, jnp.transpose(bath_ref[f, half * piece : (half + 1) * piece, :]))

    def put_index():
        column_index = jnp.transpose(index_ref[...].astype(jnp.float32))
        for f in range(frags):
            for place_of, group in enumerate((0, 2, 1, 3)):
                low = place_of * nfmax
                value = column_index[:, group * frags + f : group * frags + f + 1]
                index[f, low : low + nfmax, :] = jnp.broadcast_to(value, (nfmax, LANES)).astype(jnp.int32)

    for f in range(2):
        put_bath(f)

    loads = []
    for half in range(2):
        for slot in range(SIDE * SIDE):
            other, first = slot // SIDE, slot % SIDE
            source = slot if half == 0 else first * SIDE + other
            loads.append(
                pltpu.make_async_copy(
                    factor_ref.at[source, half], held.at[half, slot], load_sem.at[half, slot]
                )
            )
            loads[-1].start()

    def region(unit, half, second, offset, part):
        f, low, count = span(unit)
        first, other = place[half]
        if part is not None:
            count = count // 2
            low = low + part * count
        if second:
            column, width = turn(other, offset) * SIDE * piece, SIDE * piece
        else:
            column, width = (other * SIDE + turn(first, offset)) * piece, piece
        column = pl.multiple_of(column, piece)
        return initial.at[half, f, low : low + count, pl.ds(column, width)]

    messages = [(0, None, 1), (0, None, -1), (-1, 0, 1), (1, 1, -1)]
    sent = []

    def message(unit, half, second, index):
        offset, part, by = messages[index]
        where = region(unit, half, second, offset, part)
        slot = (4 if second else 0) + index
        return pltpu.make_async_remote_copy(
            src_ref=where,
            dst_ref=where,
            send_sem=send_sem.at[unit, half, slot],
            recv_sem=recv_sem.at[unit, half, slot],
            device_id=neighbour(half, second, by),
            device_id_type=MESH,
        )

    def send(unit, half, second, index):
        copy = message(unit, half, second, index)
        copy.start()
        sent.append(copy)

    def receive(unit, half, second, index):
        offset, part, by = messages[index]
        where = region(unit, half, second, offset - by, part)
        slot = (4 if second else 0) + index
        pltpu.make_async_remote_copy(
            src_ref=where,
            dst_ref=where,
            send_sem=send_sem.at[unit, half, slot],
            recv_sem=recv_sem.at[unit, half, slot],
            device_id=neighbour(half, second, by),
            device_id_type=MESH,
        ).wait_recv()

    passed = set()

    def stage(number, unit):
        if unit >= len(units) or (number, unit) in passed:
            return
        passed.add((number, unit))
        second = number > 2
        for half in range(2):
            if number == 1:
                send(unit, half, False, 0)
                send(unit, half, False, 1)
            elif number in (2, 4):
                receive(unit, half, second, 0)
                send(unit, half, second, 2)
                receive(unit, half, second, 1)
                send(unit, half, second, 3)
            elif number == 3:
                receive(unit, half, False, 2)
                receive(unit, half, False, 3)
                send(unit, half, True, 0)
                send(unit, half, True, 1)
            else:
                receive(unit, half, True, 2)
                receive(unit, half, True, 3)

    def pick(f):
        step = 8 * LANES
        lane = lax.broadcasted_iota(jnp.int32, (index.shape[1], LANES), 1) + frag * local_rows

        def one(block, total):
            start = pl.multiple_of(block * step, step)
            hot = [
                jnp.where(index[f] == lane + (start + part * LANES), 1.0, 0.0).astype(jnp.bfloat16)
                for part in range(8)
            ]
            rows = density[pl.ds(start, step), :]
            return total + jnp.dot(jnp.concatenate(hot, axis=1), rows, preferred_element_type=jnp.float32)

        total = jnp.zeros((index.shape[1], depth), jnp.float32)
        total = lax.fori_loop(0, local_rows // step, one, total)
        picked[f] = total.astype(picked.dtype).reshape(picked.shape[1:])

    def sibling_copy(f):
        return pltpu.make_async_remote_copy(
            src_ref=picked.at[f, 1 - core],
            dst_ref=summed.at[f],
            send_sem=rows_sem.at[0, f],
            recv_sem=rows_sem.at[1, f],
            device_id=sibling,
            device_id_type=MESH,
        )

    def far_copy(f):
        return pltpu.make_async_remote_copy(
            src_ref=summed.at[f, 1 - high],
            dst_ref=far.at[f],
            send_sem=rows_sem.at[2, f],
            recv_sem=rows_sem.at[3, f],
            device_id=opposite,
            device_id_type=MESH,
        )

    def send_picked(f):
        sibling_copy(f).start()

    def add_sibling(f):
        sibling_copy(f).wait()
        summed[f] = summed[f] + picked[f, core]

    def send_far(f):
        far_copy(f).start()

    def take_rows(f):
        far_copy(f).wait()
        value = summed[f, high] + far[f]
        for half in range(2):
            put(half, f, 0, value[:, half * piece : (half + 1) * piece])

    contract = (((1,), (1,)), ((), ()))

    def make_gram(f):
        total = lax.dot_general(initial[0, f], initial[0, f], contract, preferred_element_type=jnp.float32)
        total += lax.dot_general(initial[1, f], initial[1, f], contract, preferred_element_type=jnp.float32)
        gram[f] = total

    def gram_copy(f):
        return pltpu.make_async_remote_copy(
            src_ref=gram.at[f],
            dst_ref=gram_in.at[f],
            send_sem=gram_sem.at[0, f],
            recv_sem=gram_sem.at[1, f],
            device_id=partner,
            device_id_type=MESH,
        )

    share = size // ranks
    early = frags - 1

    def my_share():
        return pl.ds(pl.multiple_of(aux * share, share), share)

    def early_gram():
        total = jnp.zeros((size, size), jnp.float32)
        for half in range(2):
            first, other = place[half]
            column = pl.multiple_of((other * SIDE + first) * piece, piece)
            block = initial[half, early, :, pl.ds(column, piece)]
            total += lax.dot_general(block, block, contract, preferred_element_type=jnp.float32)
        gram[early] = total

    def share_copy(by):
        rows_of = pl.ds(pl.multiple_of(rank(by) * share, share), share)
        return pltpu.make_async_remote_copy(
            src_ref=gram.at[early, rows_of, :],
            dst_ref=shares.at[by],
            send_sem=share_sem.at[0, by],
            recv_sem=share_sem.at[1, by],
            device_id={"aux": rank(by)},
            device_id_type=MESH,
        )

    def share_swap():
        return pltpu.make_async_remote_copy(
            src_ref=shares.at[0],
            dst_ref=shares.at[ranks],
            send_sem=share_sem.at[0, 0],
            recv_sem=share_sem.at[1, 0],
            device_id=partner,
            device_id_type=MESH,
        )

    def total_copy(by, source):
        rows_of = pl.ds(pl.multiple_of(rank(source) * share, share), share)
        return pltpu.make_async_remote_copy(
            src_ref=gram_in.at[early, rows_of, :],
            dst_ref=gram_in.at[early, rows_of, :],
            send_sem=share_sem.at[2, by],
            recv_sem=share_sem.at[3, by],
            device_id={"aux": rank(by)},
            device_id_type=MESH,
        )

    def early_send():
        for by in range(1, ranks):
            share_copy(by).start()

    def early_sum():
        for by in range(1, ranks):
            share_copy(by).wait()
        total = gram[early, my_share(), :]
        for by in range(1, ranks):
            total = total + shares[by]
        shares[0] = total

    def early_swap():
        share_swap().start()

    def early_total():
        share_swap().wait()
        gram_in[early, my_share(), :] = shares[0] + shares[ranks]

    def early_spread():
        for by in range(1, ranks):
            total_copy(by, 0).start()

    def early_take():
        for by in range(1, ranks):
            total_copy(by, 0).wait_send()
            total_copy(by, -by).wait_recv()

    width = 512
    tiles_q = partial.shape[2] // width

    def project(f, low, high_row, offsets=None, unroll=False):
        count = high_row - low

        def one(q, carry):
            column = pl.ds(pl.multiple_of(q * width, width), width)
            total = jnp.zeros((count, width), jnp.float32)
            if offsets is None:
                def add(half, total):
                    block = held[half, :, :, column].reshape(SIDE * SIDE * piece, width)
                    return total + jnp.dot(
                        initial[half, f, low:high_row], block, preferred_element_type=jnp.float32
                    )

                total = lax.fori_loop(0, 2, add, total, unroll=unroll)
            for half in range(0 if offsets is None else 2):
                for offset in offsets:
                    start = turn(place[half][1], offset) * SIDE
                    block = held[half, pl.ds(start, SIDE), :, column].reshape(SIDE * piece, width)
                    columns = pl.ds(pl.multiple_of(start * piece, piece), SIDE * piece)
                    total += jnp.dot(initial[half, f, low:high_row, columns], block, preferred_element_type=jnp.float32)
            if offsets is not None and offsets[0] != 0:
                total += partial[f, low:high_row, column]
            partial[f, low:high_row, column] = total
            return carry

        lax.fori_loop(0, tiles_q, one, 0)

    row = lax.broadcasted_iota(jnp.int32, (size, size), 0)
    col = lax.broadcasted_iota(jnp.int32, (size, size), 1)

    def both_live(f):
        fragment = frag * frags + f
        used, used_bath = nfrag_ref[fragment], nbath_ref[fragment] + nfmax
        live_row = (row < used) | ((row >= nfmax) & (row < used_bath))
        live_col = (col < used) | ((col >= nfmax) & (col < used_bath))
        return live_row & live_col

    def prepare(f):
        total = gram_in[f]
        if f != early:
            gram_copy(f).wait()
            total = gram[f] + gram_in[f]
        gram_in[f] = jnp.where(both_live(f), total, jnp.where(row == col, 1.0, 0.0))

    def value_copy(f):
        return pltpu.make_async_remote_copy(
            src_ref=outgoing.at[f],
            dst_ref=incoming.at[f],
            send_sem=value_sem.at[0, f],
            recv_sem=value_sem.at[1, f],
            device_id=partner,
            device_id_type=MESH,
        )

    def mask(f):
        gram_in[f] = jnp.where(both_live(f) & (row >= col), gram_in[f], 0.0)

    def apply(f):
        theirs = gram_in[f, pl.ds(pl.multiple_of((1 - orb) * nfmax, nfmax), nfmax), :]
        mine = gram_in[f, pl.ds(pl.multiple_of(orb * nfmax, nfmax), nfmax), :]
        value = jnp.dot(theirs, partial[f], precision=HIGH, preferred_element_type=jnp.float32)
        outgoing[f] = value.astype(outgoing.dtype)
        value = jnp.dot(mine, partial[f], precision=HIGH, preferred_element_type=jnp.float32)
        value_copy(f).start()
        partial[f, :nfmax, :] = value

    def finish(f):
        value_copy(f).wait()
        out_ref[f] = (partial[f, :nfmax, :] + incoming[f].astype(jnp.float32)).astype(out_ref.dtype)

    pl.semaphore_wait(barrier, len(greeted))
    stage(1, 0)
    put_bath(2)
    fetch.wait()
    put_index()
    stage(1, 4)
    put_bath(3)
    stage(2, 0)
    stage(1, 1)
    pick(0)
    stage(3, 0)
    send_picked(0)
    pick(1)
    stage(2, 1)
    send_picked(1)
    stage(4, 0)
    add_sibling(0)
    stage(3, 1)
    send_far(0)
    stage(5, 0)
    pick(2)
    take_rows(0)
    add_sibling(1)
    send_picked(2)
    stage(1, 2)
    stage(4, 1)
    send_far(1)
    for copy in loads:
        copy.wait()
    pick(3)
    stage(2, 2)
    stage(2, 4)
    stage(3, 2)
    send_picked(3)
    take_rows(1)
    add_sibling(2)
    stage(1, 3)
    send_far(2)
    project(0, nfmax, size)
    stage(1, 6)
    stage(2, 3)
    stage(3, 3)
    stage(5, 1)
    add_sibling(3)
    take_rows(2)
    stage(4, 2)
    send_far(3)
    stage(4, 3)
    stage(1, 5)
    take_rows(3)
    stage(5, 2)
    make_gram(0)
    early_gram()
    gram_copy(0).start()
    stage(3, 4)
    early_send()
    stage(5, 3)
    project(0, 0, nfmax)
    make_gram(1)
    stage(2, 5)
    gram_copy(1).start()
    stage(1, 7)
    project(1, 0, nfmax, unroll=True)
    prepare(0)
    project(1, nfmax, size)
    early_sum()
    stage(3, 5)
    stage(4, 4)
    prepare(1)
    steps = inverse_factor(gram_in, tiles, [0,1])
    next(steps)
    next(steps)
    next(steps)
    next(steps)
    early_swap()
    next(steps)
    stage(4, 5)
    next(steps)
    stage(2, 7)
    next(steps)
    next(steps)
    stage(5, 4)
    early_total()
    stage(2, 6)
    stage(5, 5)
    early_spread()
    make_gram(2)
    stage(3, 7)
    gram_copy(2).start()
    project(2, nfmax, size, unroll=True)
    project(2, 0, nfmax, unroll=True)
    mask(0)
    early_take()
    project(3, 0, nfmax, (0,))
    mask(1)
    stage(3, 6)
    prepare(3)
    apply(0)
    prepare(2)
    steps = inverse_factor(gram_in, tiles, [2,3])
    next(steps)
    next(steps)
    apply(1)
    next(steps)
    next(steps)
    next(steps)
    stage(4, 6)
    next(steps)
    stage(4, 7)
    next(steps)
    next(steps)
    mask(2)
    apply(2)
    project(3, 0, nfmax, (-1,1))
    stage(5, 6)
    project(3, nfmax, size, unroll=True)
    stage(5, 7)
    project(3, 0, nfmax, (2,))
    mask(3)
    apply(3)
    finish(2)
    finish(0)
    finish(1)
    finish(3)
    for copy in sent:
        copy.wait_send()


def fused(nfrag, nbath, bath, density, index, factor):
    frags, depth, nbmax = bath.shape
    local_rows = density.shape[0]
    total_frags, nfmax = index.shape
    groups = total_frags // frags
    size = nfmax + nbmax
    columns = factor.shape[1]
    ranks, piece = SIDE * SIDE, depth // 2
    sems = pltpu.SemaphoreType.DMA
    half_rows = size // 2
    vmem = pltpu.VMEM
    return pl.pallas_call(
        kernel,
        out_shape=jax.ShapeDtypeStruct((frags, half_rows, columns), jnp.bfloat16),
        in_specs=[
            pl.BlockSpec(memory_space=kind)
            for kind in (pltpu.SMEM, pltpu.SMEM, vmem, pl.ANY, vmem, pl.ANY)
        ],
        out_specs=pl.BlockSpec(memory_space=vmem),
        scratch_shapes=[
            vmem((2, frags, size, ranks * piece), jnp.bfloat16),
            vmem((2, ranks, piece, columns), jnp.bfloat16),
            vmem((frags, size, columns), jnp.float32),
            vmem((frags, size, size), jnp.float32),
            vmem((frags, size, size), jnp.float32),
            vmem((2, BLOCK, LANES), jnp.float32),
            vmem((frags, half_rows, columns), jnp.bfloat16),
            vmem((frags, half_rows, columns), jnp.bfloat16),
            vmem((local_rows, depth), jnp.bfloat16),
            vmem((frags, 2, groups // 2, nfmax, depth), jnp.bfloat16),
            vmem((frags, groups // 2, nfmax, depth), jnp.bfloat16),
            vmem((frags, nfmax, depth), jnp.bfloat16),
            vmem((ranks + 1, size // ranks, size), jnp.float32),
            vmem((frags, groups * nfmax, LANES), jnp.int32),
            sems((2 * frags, 2, 8)),
            sems((2 * frags, 2, 8)),
            sems((2, ranks)),
            sems((2, frags)),
            sems((2, frags)),
            sems((4, frags)),
            sems(()),
            sems((4, ranks)),
        ],
        compiler_params=pltpu.CompilerParams(
            collective_id=0, has_side_effects=True, vmem_limit_bytes=63 * 1024 * 1024
        ),
    )(nfrag, nbath, bath, density, index, factor.reshape(ranks, 2, piece, columns))


def per_device(density, bath, factor, frag_index, nfrag, nbath):
    local_rows, _, depth = density.shape
    frags, _, _, nbmax = bath.shape
    return fused(
        nfrag, nbath, bath.reshape(frags, depth, nbmax), density.reshape(local_rows, depth), frag_index, factor
    )


def solution(mesh):
    placed = (
        P("frag", "orb", "aux"),
        P("frag", "orb", "aux", None),
        P("orb", "aux"),
        P(),
        P(),
        P(),
    )
    return jax.shard_map(
        per_device, mesh=mesh, in_specs=placed, out_specs=P("frag", "orb", "aux"), check_vma=False
    )
```
